128 devices in a mesh: leaf: 128 (over y, z, x, core).
Axes of the slice: x: 4, y: 4, z: 4, core: 2. Of those that a mesh axis runs over, the one named last changes fastest.
Arguments:
- right_hand: float32 [2048, 32, 256], P('leaf')
- leaf_live: int32 [2048], P('leaf'), may hold values from 0 to 1, as said below
- near_index: int32 [2048, 6], P('leaf'), may hold values from 0 to 2047, as said below
- near_tile: bfloat16 [2048, 6, 256, 256], P('leaf'), may hold values from -1 to 5
- far_index: int32 [2048, 8], P('leaf'), may hold values from 0 to 2047, as said below
- far_couple: bfloat16 [2048, 8, 64, 64], P('leaf'), may hold values from -0.25 to 0.25
- leaf_basis: bfloat16 [2048, 64, 256], P('leaf'), may hold values from -0.375 to 0.375
- leaf_transfer: bfloat16 [2048, 64, 64], P('leaf'), may hold values from -0.1875 to 0.1875
- tree_up: bfloat16 [254, 64, 64], replicated, may hold values from -0.5 to 0.5
- tree_couple: bfloat16 [254, 64, 64], replicated, may hold values from -0.75 to 0.75
Outputs:
- basis_next: float32 [2048, 32, 256], P('leaf')
- hessenberg: float32 [6, 32], replicated
The draws below stay inside these ranges and needn't reach their ends.
Inputs may be any that keep to these rules, and one draw needn't show every extreme that they name: `leaf_live`: each device's 16 slots hold between 5 and 16 live leaves, both counts reached on some device; which slots are live is arbitrary. `near_index`: entry 0 of each row is the row's own slot; every entry lies within 2 slots of its row's slot, and some entry lies exactly 2 away; entries may name dead slots. `far_index`: every entry lies within 16 slots of its row's slot, and some entry lies exactly 16 away; entries may name dead slots.
All inputs are finite; a program needn't handle non-finite values.
Results may differ from the reference program's by a relative error of at most 0.009.
Values may be sent and summed in bfloat16 or wider, within the bound.
No kernel may reach another device: no remote copies, remote signals or barrier semaphores. Data moves between devices by JAX's collectives and lax.ppermute only.
A program may use at most 128 MiB of HBM per device.

```python
import math
import jax
import jax.numpy as jnp
from jax import lax

P_SIZE = 256
K = 64
R = 32
NEAR = 6
FAR = 8
REACH = 2
LEAF_DEV = 16
LEAVES = 2048
NODES = 254
LEVELS = 7
N_LEAF = 128


def draw_right_hand(key, part):
    key_base = jax.random.fold_in(jax.random.fold_in(key, 11), 0)
    key_column = jax.random.fold_in(jax.random.fold_in(key, 11), 1)
    key_point = jax.random.fold_in(jax.random.fold_in(key, 11), 2)
    key_tilt = jax.random.fold_in(jax.random.fold_in(key, 11), 4)
    slot_pos = jnp.arange(LEAVES, dtype=jnp.float32) / (LEAVES - 1)
    column_scale = jnp.exp(jax.random.uniform(key_column, (R,), jnp.float32) * math.log(10.0))
    point_scale = jnp.exp(jax.random.uniform(key_point, (LEAVES, 1, P_SIZE), jnp.float32) * math.log(3.0))
    values = jax.random.normal(key_base, (LEAVES, R, P_SIZE), jnp.float32)
    power = jax.random.uniform(key_tilt, (R,), jnp.float32, 0.5, 3.0)
    rising = jnp.exp(jnp.log(1.0 + 2.0 * slot_pos)[:, None] * power[None, :])
    mean_square = (jnp.exp((2.0 * power + 1.0) * math.log(3.0)) - 1.0) / (2.0 * (2.0 * power + 1.0))
    rising = rising / jnp.sqrt(mean_square)[None, :]
    overall = 0.15 / math.sqrt(LEAVES * P_SIZE)
    return overall * values * point_scale * rising[:, :, None] * column_scale[None, :, None]


def draw_near_tile(key, part):
    key_noise, key_diag = jax.random.split(jax.random.fold_in(key, 13))
    spread = 1.0 / math.sqrt(NEAR * P_SIZE)
    slot_pos = jnp.arange(LEAVES, dtype=jnp.float32) / (LEAVES - 1)
    noise = jax.random.truncated_normal(key_noise, -4.0, 4.0, (LEAVES, NEAR, P_SIZE, P_SIZE), jnp.float32) * spread
    weights = jnp.exp(math.log(0.15) + jax.random.uniform(key_diag, (LEAVES, P_SIZE), jnp.float32) * math.log(10.0))
    trend = 0.3 + 1.7 * slot_pos
    smoothing = weights * trend[:, None]
    own_tile = (jnp.arange(NEAR) == 0)[None, :, None, None]
    on_diagonal = (jnp.arange(P_SIZE)[:, None] == jnp.arange(P_SIZE)[None, :])[None, None, :, :]
    tiles = noise + jnp.where(own_tile & on_diagonal, smoothing[:, None, None, :], 0.0)
    return tiles.astype(jnp.bfloat16)


def draw_leaf_live(key, part):
    key_count, key_full, key_empty, key_perm = jax.random.split(jax.random.fold_in(key, 3), 4)
    lowest = max(1, LEAF_DEV // 3)
    counts = jax.random.randint(key_count, (N_LEAF,), lowest, LEAF_DEV + 1)
    full_dev = jax.random.randint(key_full, (), 0, N_LEAF)
    empty_dev = (full_dev + 1 + jax.random.randint(key_empty, (), 0, N_LEAF - 1)) % N_LEAF
    counts = counts.at[full_dev].set(LEAF_DEV).at[empty_dev].set(lowest)
    ranks = jax.vmap(lambda subkey: jax.random.permutation(subkey, LEAF_DEV))(jax.random.split(key_perm, N_LEAF))
    return (ranks < counts[:, None]).astype(jnp.int32).reshape(-1)


def draw_near_index(key, part):
    offsets = jax.random.randint(jax.random.fold_in(key, 5), (LEAVES, NEAR), -REACH, REACH + 1)
    offsets = offsets.at[:, 0].set(0).at[LEAF_DEV, 1].set(-REACH)
    rows = jnp.arange(LEAVES, dtype=jnp.int32)[:, None]
    return jnp.clip(rows + offsets, 0, LEAVES - 1).astype(jnp.int32)


def draw_far_index(key, part):
    key_size, key_sign = jax.random.split(jax.random.fold_in(key, 7))
    magnitude = jax.random.randint(key_size, (LEAVES, FAR), REACH + 1, LEAF_DEV + 1)
    signs = jax.random.randint(key_sign, (LEAVES, FAR), 0, 2) * 2 - 1
    offsets = magnitude * signs
    offsets = offsets.at[LEAF_DEV, 0].set(-LEAF_DEV).at[LEAVES - 1 - LEAF_DEV, 0].set(LEAF_DEV)
    rows = jnp.arange(LEAVES, dtype=jnp.int32)[:, None]
    return jnp.clip(rows + offsets, 0, LEAVES - 1).astype(jnp.int32)


def block_scale(rng, shape, cuts, least, largest):
    factor_of = 1.0
    for axis_at, shards_of in cuts:
        draws = jax.random.uniform(jax.random.fold_in(jax.random.fold_in(rng, 6), axis_at), (shards_of,), jnp.float32, least / len(cuts), largest / len(cuts))
        factor_of = factor_of * jnp.repeat(jnp.exp(draws), shape[axis_at] // shards_of).reshape((-1,) + (1,) * (len(shape) - 1 - axis_at))
    return factor_of


def centred(stream_key, shape, deviation, limit, cuts=(), kind=jnp.bfloat16):
    entries = deviation * jax.random.normal(stream_key, shape, jnp.float32)
    if cuts:
        entries = entries * block_scale(stream_key, shape, cuts, -0.22, 0.18)
    return jnp.clip(entries, -limit, limit).astype(kind)


def setup_inputs(seed: int = 0) -> dict:
    streams_of = jax.random.split(jax.random.key(seed), 11)
    right_hand = draw_right_hand(jax.random.fold_in(streams_of[10], 71), 0)
    leaf_live = draw_leaf_live(jax.random.fold_in(streams_of[10], 71), 0)
    near_index = draw_near_index(jax.random.fold_in(streams_of[10], 71), 0)
    near_tile = draw_near_tile(jax.random.fold_in(streams_of[10], 71), 0)
    far_index = draw_far_index(jax.random.fold_in(streams_of[10], 71), 0)
    far_couple = centred(streams_of[5], (LEAVES, FAR, K, K), (FAR * K) ** -0.5, 0.25, ((0, 128),))
    leaf_basis = centred(streams_of[6], (LEAVES, K, P_SIZE), P_SIZE ** -0.5, 0.375, ((0, 128),))
    leaf_transfer = centred(streams_of[7], (LEAVES, K, K), (LEAF_DEV * K) ** -0.5, 0.1875, ((0, 128),))
    tree_up = centred(streams_of[8], (NODES, K, K), (2 * K) ** -0.5, 0.5)
    tree_couple = centred(streams_of[9], (NODES, K, K), K ** -0.5, 0.75)
    return dict(right_hand=right_hand, leaf_live=leaf_live, near_index=near_index, near_tile=near_tile, far_index=far_index, far_couple=far_couple, leaf_basis=leaf_basis, leaf_transfer=leaf_transfer, tree_up=tree_up, tree_couple=tree_couple)


epsilon = 1e-06

def level_start(level):
    return 2 * N_LEAF - 2 * (N_LEAF >> level)

def apply_operator(vector, leaf_live, near_index, near_tile, far_index, far_couple, leaf_basis, leaf_transfer, tree_up, tree_couple):
    live_mask = leaf_live.astype(jnp.float32)[:, None, None]
    inputs = (vector * live_mask).astype(jnp.bfloat16)

    def near_block(pieces):
        block_index, block_tiles = pieces
        columns = inputs[block_index].astype(jnp.float32)
        return jnp.einsum('inrp,inpq->irq', columns, block_tiles.astype(jnp.float32))
    near = lax.map(near_block, (near_index.reshape(N_LEAF, LEAF_DEV, NEAR), near_tile.reshape(N_LEAF, LEAF_DEV, NEAR, P_SIZE, P_SIZE)))
    near = near.reshape(LEAVES, R, P_SIZE)
    moments = jnp.einsum('irp,ikp->irk', inputs.astype(jnp.float32), leaf_basis.astype(jnp.float32)).astype(jnp.bfloat16)
    far_term = jnp.einsum('ifrk,ifkj->irj', moments[far_index].astype(jnp.float32), far_couple.astype(jnp.float32))
    transfer_dev = leaf_transfer.reshape(N_LEAF, LEAF_DEV, K, K).astype(jnp.float32)
    coarse = jnp.einsum('dirk,dikj->drj', moments.reshape(N_LEAF, LEAF_DEV, R, K).astype(jnp.float32), transfer_dev).astype(jnp.bfloat16)
    locals_list = []
    for level in range(LEVELS):
        width_now = N_LEAF >> level
        first = level_start(level)
        swapped = coarse.reshape(width_now // 2, 2, R, K)[:, ::-1].reshape(width_now, R, K)
        locals_list.append(jnp.einsum('nrk,nkj->nrj', swapped.astype(jnp.float32), tree_couple[first:first + width_now].astype(jnp.float32)))
        lifted = jnp.einsum('nrk,nkj->nrj', coarse.astype(jnp.float32), tree_up[first:first + width_now].astype(jnp.float32))
        coarse = (lifted[0::2] + lifted[1::2]).astype(jnp.bfloat16)
    downward = jnp.zeros((1, R, K), jnp.bfloat16)
    for level in reversed(range(LEVELS)):
        width_now = N_LEAF >> level
        first = level_start(level)
        parent = jnp.repeat(downward, 2, axis=0)
        carried = jnp.einsum('nrj,nkj->nrk', parent.astype(jnp.float32), tree_up[first:first + width_now].astype(jnp.float32))
        downward = (locals_list[level] + carried).astype(jnp.bfloat16)
    leaf_down = jnp.einsum('drj,dikj->dirk', downward.astype(jnp.float32), transfer_dev).reshape(LEAVES, R, K)
    local_total = (far_term + leaf_down).astype(jnp.bfloat16)
    spread = jnp.einsum('irk,ikp->irp', local_total.astype(jnp.float32), leaf_basis.astype(jnp.float32))
    return live_mask * (near + spread)

def column_sums(first_field, second_field):
    return lax.optimization_barrier(jnp.sum(first_field * second_field, axis=(0, 2)))

def reference(right_hand, leaf_live, near_index, near_tile, far_index, far_couple, leaf_basis, leaf_transfer, tree_up, tree_couple):

    def operator(vector):
        return apply_operator(vector, leaf_live, near_index, near_tile, far_index, far_couple, leaf_basis, leaf_transfer, tree_up, tree_couple)
    live_mask = leaf_live.astype(jnp.float32)[:, None, None]
    start_vec = right_hand * live_mask
    norm_start = jnp.sqrt(column_sums(start_vec, start_vec) + epsilon)
    basis_one = start_vec / norm_start[None, :, None]
    image_one = operator(basis_one)
    first_inner = column_sums(basis_one, image_one)
    residue_one = image_one - first_inner[None, :, None] * basis_one
    first_length = jnp.sqrt(column_sums(residue_one, residue_one) + epsilon)
    basis_two = residue_one / first_length[None, :, None]
    image_two = operator(basis_two)
    cross_inner = column_sums(basis_one, image_two)
    self_inner = column_sums(basis_two, image_two)
    residue_two = image_two - cross_inner[None, :, None] * basis_one - self_inner[None, :, None] * basis_two
    second_length = jnp.sqrt(column_sums(residue_two, residue_two) + epsilon)
    basis_next = residue_two / second_length[None, :, None]
    hessenberg = jnp.stack([norm_start, first_inner, first_length, cross_inner, self_inner, second_length])
    return (basis_next, hessenberg)
```

```python
import functools

import jax
import jax.numpy as jnp
from jax import lax
from jax.experimental import pallas as pl
from jax.experimental.pallas import tpu as pltpu
from jax.sharding import PartitionSpec as P

EPSILON = 1e-06
F32 = jnp.float32
BF16 = jnp.bfloat16
NT = (((1,), (1,)), ((), ()))

VMEM = pl.BlockSpec(memory_space=pltpu.VMEM)
SMEM = pl.BlockSpec(memory_space=pltpu.SMEM)
ANY = pl.BlockSpec(memory_space=pl.ANY)

SLOTS, RHS, POINTS, RANK = 16, 32, 256, 64
REACH = 2
HALF = SLOTS // 2
MOM_ROWS = HALF * RHS
NEAR_ROWS = REACH * 2 * RHS
BOX_AT = MOM_ROWS + NEAR_ROWS
PAIR_ROWS = BOX_AT + RHS
DEVICES = 128
LEVELS = 7
CHIPS = DEVICES // 2


def dot(a, b):
    return jnp.dot(a, b, preferred_element_type=F32)


def dot_nt(a, b):
    return lax.dot_general(a, b, NT, preferred_element_type=F32)


def row_sum(x):
    return jnp.sum(x, axis=1, keepdims=True)


def lanes(shape=(RHS, 128)):
    return lax.broadcasted_iota(jnp.int32, shape, 1)


def rows(shape=(RHS, 128)):
    return lax.broadcasted_iota(jnp.int32, shape, 0)


def level_start(level):
    return 2 * DEVICES - 2 * (DEVICES >> level)


def three_parts(column):
    high = column.astype(BF16).astype(F32)
    rest = column - high
    middle = rest.astype(BF16).astype(F32)
    low = (rest - middle).astype(BF16).astype(F32)
    return high, middle, low


def message(moment, sums):
    block = jnp.concatenate([moment.astype(F32), jnp.zeros((RHS, 128 - RANK), F32)], axis=1)
    at = lanes()
    for j, column in enumerate(sums):
        for k, part in enumerate(three_parts(column)):
            block = jnp.where(at == RANK + 3 * j + k, part, block)
    return block.astype(BF16)


def read_sum(block, j):
    at = lanes()
    first = RANK + 3 * j
    return row_sum(jnp.where((at >= first) & (at < first + 3), block, 0.0))


def pack_out(inputs, moments, box, sums, pa_ref, pb_ref, own_ref):
    block = message(box.astype(BF16), sums)
    own_ref[...] = block
    pa_ref[BOX_AT:PAIR_ROWS, :] = block
    for g in range(HALF):
        both = jnp.concatenate([moments[g], moments[g + HALF]], axis=1).astype(BF16)
        pa_ref[g * RHS : (g + 1) * RHS, :] = both
        pb_ref[g * RHS : (g + 1) * RHS, :] = both
    odd = lax.rem(lax.axis_index("leaf"), 2)

    def edge(ref, first):
        for j in range(REACH):
            x = inputs[first + j]
            for half in range(2):
                start = MOM_ROWS + (2 * j + half) * RHS
                ref[start : start + RHS, :] = x[:, half * 128 : (half + 1) * 128]

    @pl.when(odd == 0)
    def _():
        edge(pa_ref, SLOTS - REACH)
        edge(pb_ref, 0)

    @pl.when(odd == 1)
    def _():
        edge(pa_ref, 0)
        edge(pb_ref, SLOTS - REACH)


def up_moments(inputs, basis_ref, transfer_ref):
    moments = []
    box = jnp.zeros((RHS, RANK), F32)
    for g in range(SLOTS):
        moment = dot_nt(inputs[g], basis_ref[g]).astype(BF16)
        moments.append(moment.astype(F32))
        box = box + dot(moment, transfer_ref[g])
    return moments, box


def first_kernel(live_ref, rh_ref, basis_ref, transfer_ref, pa_ref, pb_ref, own_ref, sb_ref):
    inputs = []
    square = jnp.zeros((RHS, POINTS), F32)
    for g in range(SLOTS):
        s = rh_ref[g] * live_ref[g].astype(F32)
        square = square + s * s
        sb = s.astype(BF16)
        sb_ref[g] = sb
        inputs.append(sb)
    moments, box = up_moments(inputs, basis_ref, transfer_ref)
    pack_out(inputs, moments, box, [row_sum(square)], pa_ref, pb_ref, own_ref)


def pair_kernel(n_sums, own_ref, ra_ref, up_ref, out_ref, up_vmem, sem):
    position = lax.axis_index("leaf")
    odd = lax.rem(position, 2)
    first = pl.multiple_of((position - odd) * RANK, 2 * RANK)
    copy = pltpu.make_async_copy(up_ref.at[pl.ds(first, 2 * RANK)], up_vmem, sem)
    copy.start()
    own = own_ref[...].astype(F32)
    other = ra_ref[BOX_AT:PAIR_ROWS, :].astype(F32)
    even_side = jnp.where(odd == 0, own, other)
    odd_side = jnp.where(odd == 0, other, own)
    both = own + other
    sums = [read_sum(both, j) for j in range(n_sums)]
    joined = jnp.concatenate([even_side[:, :RANK], odd_side[:, :RANK]], axis=1).astype(BF16)
    copy.wait()
    block = message(dot(joined, up_vmem[...]).astype(BF16), sums)
    for c in range(CHIPS):
        out_ref[c] = block


def near_far_kernel(
    step_leaves,
    near_index_ref,
    far_index_ref,
    sb_ref,
    own_ref,
    ra_ref,
    rb_ref,
    tile_ref,
    couple_ref,
    near_ref,
    far_ref,
    x_ref,
    left_ref,
    right_ref,
):
    step = pl.program_id(0)
    position = lax.axis_index("leaf")
    odd = lax.rem(position, 2)

    @pl.when(step == 0)
    def _():
        at = lanes()

        def spread_moments(source, first):
            for g in range(HALF):
                both = source[g * RHS : (g + 1) * RHS, :].astype(F32)
                turned = pltpu.roll(both, RANK, 1)
                low = at < RANK
                left_ref[first + g] = jnp.where(low, both, 0.0).astype(BF16)
                right_ref[first + g] = jnp.where(low, 0.0, turned).astype(BF16)
                left_ref[first + HALF + g] = jnp.where(low, turned, 0.0).astype(BF16)
                right_ref[first + HALF + g] = jnp.where(low, 0.0, both).astype(BF16)

        def edges(source, first):
            for j in range(REACH):
                for half in range(2):
                    start = MOM_ROWS + (2 * j + half) * RHS
                    x_ref[first + j, :, half * 128 : (half + 1) * 128] = source[
                        start : start + RHS, :
                    ]

        spread_moments(own_ref, SLOTS)
        for g in range(SLOTS):
            x_ref[REACH + g] = sb_ref[g]

        @pl.when(odd == 0)
        def _():
            spread_moments(rb_ref, 0)
            spread_moments(ra_ref, 2 * SLOTS)
            edges(rb_ref, 0)
            edges(ra_ref, REACH + SLOTS)

        @pl.when(odd == 1)
        def _():
            spread_moments(ra_ref, 0)
            spread_moments(rb_ref, 2 * SLOTS)
            edges(ra_ref, 0)
            edges(rb_ref, REACH + SLOTS)

    near_base = position * SLOTS - REACH
    far_base = position * SLOTS - SLOTS
    for j in range(step_leaves):
        g = step * step_leaves + j
        columns = [x_ref[near_index_ref[g, k] - near_base] for k in range(6)]
        near_ref[j] = dot(jnp.concatenate(columns, axis=1), tile_ref[j])
        pairs = [
            left_ref[far_index_ref[g, 2 * f] - far_base]
            + right_ref[far_index_ref[g, 2 * f + 1] - far_base]
            for f in range(4)
        ]
        far_ref[j] = dot(jnp.concatenate(pairs, axis=1), couple_ref[j])


def tree_sweep(own_ref, ra_ref, gathered_ref, up_ref, couple_ref, nodes_ref, couple_vmem, sems):
    position = lax.axis_index("leaf")
    copies = []
    for level in range(LEVELS):
        node = level_start(level) + (position >> level)
        start = pl.multiple_of(node * RANK, RANK)
        copy = pltpu.make_async_copy(
            couple_ref.at[pl.ds(start, RANK)], couple_vmem.at[level], sems.at[level]
        )
        copy.start()
        copies.append(copy)
    total = gathered_ref[0].astype(F32)
    for c in range(1, CHIPS):
        total = total + gathered_ref[c].astype(F32)
    current = [gathered_ref[c][:, :RANK] for c in range(CHIPS)]
    for level in range(1, LEVELS):
        first = level_start(level) - DEVICES
        for n in range(len(current)):
            nodes_ref[first + n] = current[n]
        if level + 1 < LEVELS:
            following = []
            for m in range(len(current) // 2):
                start = (level_start(level) + 2 * m) * RANK
                joined = jnp.concatenate([current[2 * m], current[2 * m + 1]], axis=1)
                following.append(dot(joined, up_ref[start : start + 2 * RANK, :]).astype(BF16))
            current = following
    locals_list = []
    for level in range(LEVELS):
        if level == 0:
            sibling = ra_ref[BOX_AT:PAIR_ROWS, :][:, :RANK]
        else:
            sibling = nodes_ref[level_start(level) - DEVICES + ((position >> level) ^ 1)]
        copies[level].wait()
        locals_list.append(dot(sibling, couple_vmem[level]))
    downward = locals_list[LEVELS - 1].astype(BF16)
    for level in reversed(range(LEVELS - 1)):
        node = level_start(level) + (position >> level)
        up = up_ref[pl.ds(pl.multiple_of(node * RANK, RANK), RANK), :]
        downward = (locals_list[level] + dot_nt(downward, up)).astype(BF16)
    return downward, total


def image_of(g, downward, live_ref, near_ref, far_ref, basis_ref, transfer_ref):
    leaf_down = dot_nt(downward, transfer_ref[g])
    local_total = (far_ref[g] + leaf_down).astype(BF16)
    return live_ref[g].astype(F32) * (near_ref[g] + dot(local_total, basis_ref[g]))


def middle_kernel(
    live_ref,
    rh_ref,
    basis_ref,
    transfer_ref,
    own_in_ref,
    ra_ref,
    gathered_ref,
    up_ref,
    couple_ref,
    near_ref,
    far_ref,
    pa_ref,
    pb_ref,
    own_ref,
    sb_ref,
    image_ref,
    scal_ref,
    nodes_ref,
    couple_vmem,
    sems,
):
    downward, total = tree_sweep(
        own_in_ref, ra_ref, gathered_ref, up_ref, couple_ref, nodes_ref, couple_vmem, sems
    )
    square = read_sum(total, 0)
    norm = jnp.sqrt(square + EPSILON)
    scal_ref[...] = jnp.where(lanes() == 0, norm, square)
    inputs = []
    inner = jnp.zeros((RHS, POINTS), F32)
    length = jnp.zeros((RHS, POINTS), F32)
    for g in range(SLOTS):
        image = image_of(g, downward, live_ref, near_ref, far_ref, basis_ref, transfer_ref) / norm
        image_ref[g] = image
        basis_one = rh_ref[g] * live_ref[g].astype(F32) / norm
        inner = inner + basis_one * image
        length = length + image * image
        sb = image.astype(BF16)
        sb_ref[g] = sb
        inputs.append(sb)
    moments, box = up_moments(inputs, basis_ref, transfer_ref)
    pack_out(inputs, moments, box, [row_sum(inner), row_sum(length)], pa_ref, pb_ref, own_ref)


def as_row(column, shift):
    return jnp.sum(jnp.where(lanes() == rows() + shift, column, 0.0), axis=0, keepdims=True)


def as_column(row, shift):
    return row_sum(jnp.where(lanes() == rows() + shift, row, 0.0))


def last_operator_kernel(
    live_ref,
    rh_ref,
    basis_ref,
    transfer_ref,
    own_in_ref,
    ra_ref,
    gathered_ref,
    up_ref,
    couple_ref,
    near_ref,
    far_ref,
    image_ref,
    scal_in_ref,
    one_ref,
    two_ref,
    v_ref,
    send_ref,
    scal_ref,
    nodes_ref,
    couple_vmem,
    sems,
):
    downward, total = tree_sweep(
        own_in_ref, ra_ref, gathered_ref, up_ref, couple_ref, nodes_ref, couple_vmem, sems
    )
    norm = scal_in_ref[:, 0:1]
    one_one = (scal_in_ref[:, 1:2] / norm) / norm
    first_inner = read_sum(total, 0)
    image_square = read_sum(total, 1)
    residue = image_square - 2.0 * first_inner * first_inner + first_inner * first_inner * one_one
    residue = jnp.maximum(residue, 0.0)
    first_length = jnp.sqrt(residue + EPSILON)
    one_two = (first_inner - first_inner * one_one) / first_length
    two_two = (residue / first_length) / first_length
    at = lanes()
    scal = jnp.zeros((RHS, 128), F32)
    for j, column in enumerate((norm, first_inner, first_length, one_one, one_two, two_two)):
        scal = jnp.where(at == j, column, scal)
    scal_ref[...] = scal
    cross = jnp.zeros((RHS, POINTS), F32)
    own = jnp.zeros((RHS, POINTS), F32)
    square = jnp.zeros((RHS, POINTS), F32)
    for g in range(SLOTS):
        image = image_ref[g]
        y = image_of(g, downward, live_ref, near_ref, far_ref, basis_ref, transfer_ref)
        basis_one = rh_ref[g] * live_ref[g].astype(F32) / norm
        basis_two = (image - first_inner * basis_one) / first_length
        v = (y - first_inner * image) / first_length
        one_ref[g] = basis_one
        two_ref[g] = basis_two
        v_ref[g] = v
        cross = cross + basis_one * v
        own = own + basis_two * v
        square = square + v * v
    row = as_row(row_sum(cross), 0) + as_row(row_sum(own), 32) + as_row(row_sum(square), 64)
    for d in range(DEVICES):
        send_ref[d] = row


def final_kernel(one_ref, two_ref, v_ref, scal_ref, gathered_ref, next_ref, hess_ref):
    row = jnp.sum(gathered_ref[...], axis=0)
    cross, own, square = as_column(row, 0), as_column(row, 32), as_column(row, 64)
    norm, first_inner, first_length, one_one, one_two, two_two = (
        scal_ref[:, j : j + 1] for j in range(6)
    )
    residue = (
        square
        - 2.0 * cross * cross
        - 2.0 * own * own
        + cross * cross * one_one
        + own * own * two_two
        + 2.0 * cross * own * one_two
    )
    second_length = jnp.sqrt(jnp.maximum(residue, 0.0) + EPSILON)
    for j, column in enumerate((norm, first_inner, first_length, cross, own, second_length)):
        hess_ref[j : j + 1, :] = as_row(column, 0)[:, :RHS]
    for g in range(SLOTS):
        next_ref[g] = (v_ref[g] - cross * one_ref[g] - own * two_ref[g]) / second_length


def shape(dims, dtype):
    return jax.ShapeDtypeStruct(dims, dtype)


FIELD = (SLOTS, RHS, POINTS)
PACKED = [shape((PAIR_ROWS, 128), BF16), shape((BOX_AT, 128), BF16), shape((RHS, 128), BF16)]
TREE_SCRATCH = [
    pltpu.VMEM((DEVICES - 2, RHS, RANK), BF16),
    pltpu.VMEM((LEVELS, RANK, RANK), BF16),
    pltpu.SemaphoreType.DMA((LEVELS,)),
]
MIB = 1 << 20


def params(mib):
    return pltpu.CompilerParams(vmem_limit_bytes=mib * MIB)


def on_device(
    right_hand,
    leaf_live,
    near_index,
    near_tile,
    far_index,
    far_couple,
    leaf_basis,
    leaf_transfer,
    tree_up,
    tree_couple,
):
    up_rows = tree_up.reshape(-1, RANK)
    couple_rows = tree_couple.reshape(-1, RANK)
    tiles = near_tile.reshape(SLOTS, 6 * POINTS, POINTS)
    couples = far_couple.reshape(SLOTS, 8 * RANK, RANK)
    same = [(i, i ^ 1) for i in range(DEVICES)]
    across = [(i, i + 1) for i in range(1, DEVICES - 1, 2)]
    across += [(j, i) for i, j in across]
    groups = [[2 * c + core for c in range(CHIPS)] for core in range(2)]

    def exchange(pa, pb, own, n_sums):
        ra = lax.ppermute(pa, "leaf", same)
        rb = lax.ppermute(pb, "leaf", across)
        sent = pl.pallas_call(
            functools.partial(pair_kernel, n_sums),
            out_shape=shape((CHIPS, RHS, 128), BF16),
            in_specs=[VMEM, VMEM, ANY],
            out_specs=VMEM,
            scratch_shapes=[pltpu.VMEM((2 * RANK, RANK), BF16), pltpu.SemaphoreType.DMA],
            compiler_params=params(4),
            name="pair",
        )(own, ra, up_rows)
        gathered = lax.all_to_all(sent, "leaf", 0, 0, axis_index_groups=groups)
        return ra, rb, gathered

    def near_far(sb, pb, ra, rb):
        leaves = 2
        whole = lambda dims: pl.BlockSpec(dims, lambda i: (0,) * len(dims))
        part = lambda dims: pl.BlockSpec((leaves, *dims), lambda i: (i, 0, 0))
        return pl.pallas_call(
            functools.partial(near_far_kernel, leaves),
            grid=(SLOTS // leaves,),
            out_shape=[shape(FIELD, F32), shape((SLOTS, RHS, RANK), F32)],
            in_specs=[
                SMEM,
                SMEM,
                whole(FIELD),
                whole((BOX_AT, 128)),
                whole((PAIR_ROWS, 128)),
                whole((BOX_AT, 128)),
                part((6 * POINTS, POINTS)),
                part((8 * RANK, RANK)),
            ],
            out_specs=[part((RHS, POINTS)), part((RHS, RANK))],
            scratch_shapes=[
                pltpu.VMEM((SLOTS + 2 * REACH, RHS, POINTS), BF16),
                pltpu.VMEM((3 * SLOTS, RHS, 128), BF16),
                pltpu.VMEM((3 * SLOTS, RHS, 128), BF16),
            ],
            compiler_params=params(16),
            cost_estimate=pl.CostEstimate(
                flops=1_000_000_000, bytes_accessed=16_000_000, transcendentals=0
            ),
            name="near_far",
        )(near_index, far_index, sb, pb, ra, rb, tiles, couples)

    pa, pb, own, sb = pl.pallas_call(
        first_kernel,
        out_shape=[*PACKED, shape(FIELD, BF16)],
        in_specs=[SMEM, VMEM, VMEM, VMEM],
        out_specs=[VMEM] * 4,
        compiler_params=params(8),
        name="first",
    )(leaf_live, right_hand, leaf_basis, leaf_transfer)
    ra, rb, gathered = exchange(pa, pb, own, 1)
    near, far = near_far(sb, pb, ra, rb)
    pa, pb, own, sb, image, scal = pl.pallas_call(
        middle_kernel,
        out_shape=[*PACKED, shape(FIELD, BF16), shape(FIELD, F32), shape((RHS, 128), F32)],
        in_specs=[SMEM] + [VMEM] * 7 + [ANY] + [VMEM] * 2,
        out_specs=[VMEM] * 6,
        scratch_shapes=TREE_SCRATCH,
        compiler_params=params(24),
        name="middle",
    )(
        leaf_live, right_hand, leaf_basis, leaf_transfer, own, ra, gathered,
        up_rows, couple_rows, near, far,
    )
    ra, rb, gathered = exchange(pa, pb, own, 2)
    near, far = near_far(sb, pb, ra, rb)
    one, two, v, sent, scal = pl.pallas_call(
        last_operator_kernel,
        out_shape=[shape(FIELD, F32)] * 3
        + [shape((DEVICES, 1, 128), F32), shape((RHS, 128), F32)],
        in_specs=[SMEM] + [VMEM] * 7 + [ANY] + [VMEM] * 4,
        out_specs=[VMEM] * 5,
        scratch_shapes=TREE_SCRATCH,
        compiler_params=params(24),
        name="last_operator",
    )(
        leaf_live, right_hand, leaf_basis, leaf_transfer, own, ra, gathered,
        up_rows, couple_rows, near, far, image, scal,
    )
    gathered = lax.all_to_all(sent, "leaf", 0, 0)
    return pl.pallas_call(
        final_kernel,
        out_shape=[shape(FIELD, F32), shape((6, RHS), F32)],
        in_specs=[VMEM] * 5,
        out_specs=[VMEM] * 2,
        compiler_params=params(8),
        name="final",
    )(one, two, v, scal, gathered)


def solution(mesh):
    placed = (
        P("leaf", None, None),
        P("leaf"),
        P("leaf", None),
        P("leaf", None, None, None),
        P("leaf", None),
        P("leaf", None, None, None),
        P("leaf", None, None),
        P("leaf", None, None),
        P(),
        P(),
    )
    return jax.shard_map(
        on_device,
        mesh=mesh,
        in_specs=placed,
        out_specs=(P("leaf", None, None), P()),
        check_vma=False,
    )
```

```python
import functools

import jax
import jax.numpy as jnp
from jax import lax
from jax.experimental import pallas as pl
from jax.experimental.pallas import tpu as pltpu
from jax.sharding import PartitionSpec as P


EPSILON = 1e-06
F32 = jnp.float32
BF16 = jnp.bfloat16
NT = (((1,), (1,)), ((), ()))

SMEM = pl.BlockSpec(memory_space=pltpu.SMEM)
ANY = pl.BlockSpec(memory_space=pl.ANY)
VMEM = pl.BlockSpec(memory_space=pltpu.VMEM)
HBM = pl.BlockSpec(memory_space=pltpu.HBM)

SLOTS, RHS, POINTS, RANK = 16, 32, 256, 64
REACH = 2
HALF = SLOTS // 2
MOM_ROWS = HALF * RHS
NEAR_ROWS = REACH * 2 * RHS
BOX_AT = MOM_ROWS + NEAR_ROWS
PAIR_ROWS = BOX_AT + RHS
DEVICES = 128
LEVELS = 7
CHIPS = DEVICES // 2
NODES = 254
TURN = 16
DEPTH = 4
COPIES = 8
UP_NODES = 16
UP_PARTS = CHIPS // UP_NODES + 1


def dot(a, b):
    return jnp.dot(a, b, preferred_element_type=F32)


def dot_nt(a, b):
    return lax.dot_general(a, b, NT, preferred_element_type=F32)


def row_sum(x):
    return jnp.sum(x, axis=1, keepdims=True)


def lanes(shape=(RHS, 128)):
    return lax.broadcasted_iota(jnp.int32, shape, 1)


def rows(shape=(RHS, 128)):
    return lax.broadcasted_iota(jnp.int32, shape, 0)


def level_start(level):
    return 2 * DEVICES - 2 * (DEVICES >> level)


def three_parts(column):
    high = column.astype(BF16).astype(F32)
    rest = column - high
    middle = rest.astype(BF16).astype(F32)
    low = (rest - middle).astype(BF16).astype(F32)
    return high, middle, low


def message(moment, sums):
    block = jnp.concatenate([moment.astype(F32), jnp.zeros((RHS, 128 - RANK), F32)], axis=1)
    at = lanes()
    for j, column in enumerate(sums):
        for k, part in enumerate(three_parts(column)):
            block = jnp.where(at == RANK + 3 * j + k, part, block)
    return block.astype(BF16)


def read_sum(block, j):
    at = lanes()
    first = RANK + 3 * j
    return row_sum(jnp.where((at >= first) & (at < first + 3), block, 0.0))


def pack_out(inputs, moments, box, sums, pa_ref, pb_ref, own_ref):
    block = message(box.astype(BF16), sums)
    own_ref[...] = block
    pa_ref[BOX_AT:PAIR_ROWS, :] = block
    for j in range(HALF):
        both = moments[:, j * 128 : (j + 1) * 128]
        pa_ref[j * RHS : (j + 1) * RHS, :] = both
        pb_ref[j * RHS : (j + 1) * RHS, :] = both
    odd = lax.rem(lax.axis_index("leaf"), 2)

    def edge(ref, first):
        for j in range(REACH):
            x = inputs[first + j]
            for half in range(2):
                start = MOM_ROWS + (2 * j + half) * RHS
                ref[start : start + RHS, :] = x[:, half * 128 : (half + 1) * 128]

    @pl.when(odd == 0)
    def _():
        edge(pa_ref, SLOTS - REACH)
        edge(pb_ref, 0)

    @pl.when(odd == 1)
    def _():
        edge(pa_ref, 0)
        edge(pb_ref, SLOTS - REACH)


def block_of_lane():
    return lanes((RHS, 4 * RANK)) // RANK


def up_moments(inputs, basis_ref, transfer_ref):
    block = block_of_lane()
    groups = []
    for q in range(SLOTS // 4):
        four = jnp.concatenate(inputs[4 * q : 4 * q + 4], axis=0)
        crossed = dot_nt(four, basis_ref[4 * q * RANK : 4 * (q + 1) * RANK, :])
        group = crossed[0:RHS, :]
        for j in range(1, 4):
            group = jnp.where(block == j, crossed[j * RHS : (j + 1) * RHS, :], group)
        groups.append(group.astype(BF16))
    moments = jnp.concatenate(groups, axis=1)
    return moments, dot(moments, transfer_ref[...])


def start_copies(sources, targets, sems):
    copies = [
        pltpu.make_async_copy(source, target, sems.at[i])
        for i, (source, target) in enumerate(zip(sources, targets, strict=True))
    ]
    for copy in copies:
        copy.start()
    return copies


def one_hot(count, nodes):
    at, row = lanes((count, NODES)), rows((count, NODES))
    block = jnp.zeros((count, NODES), F32)
    for i, node in enumerate(nodes):
        block = jnp.where((row == i) & (at == node), 1.0, block)
    return block.astype(BF16)


def first_kernel(
    live_hbm,
    rh_hbm,
    basis_hbm,
    transfer_hbm,
    up_hbm,
    pa_ref,
    pb_ref,
    own_ref,
    sb_hbm,
    mom_hbm,
    pair_ref,
    live_ref,
    rh_ref,
    basis_ref,
    transfer_ref,
    up_ref,
    sb_ref,
    turn_ref,
    sems,
    out_sems,
):
    live_in, *copies = start_copies(
        (live_hbm, rh_hbm, basis_hbm, transfer_hbm, up_hbm),
        (live_ref, rh_ref, basis_ref, transfer_ref, up_ref),
        sems,
    )
    live_in.wait()
    copies[0].wait()
    inputs = []
    square = jnp.zeros((RHS, POINTS), F32)
    for g in range(SLOTS):
        s = rh_ref[g] * live_ref[g].astype(F32)
        square = square + s * s
        sb = s.astype(BF16)
        sb_ref[g] = sb
        inputs.append(sb)
    sb_out = pltpu.make_async_copy(sb_ref, sb_hbm, out_sems.at[0])
    sb_out.start()
    copies[1].wait()
    copies[2].wait()
    moments, box = up_moments(inputs, basis_ref, transfer_ref)
    pack_out(inputs, moments, box, [row_sum(square)], pa_ref, pb_ref, own_ref)
    mom_out = pltpu.make_async_copy(pb_ref.at[pl.ds(0, MOM_ROWS)], mom_hbm, out_sems.at[1])
    mom_out.start()
    position = lax.axis_index("leaf")
    first = position - lax.rem(position, 2)
    pick = one_hot(8, (first, first + 1))
    copies[3].wait()
    for k in range(0, RANK, 4):
        four = dot_nt(pick, up_ref[k * RANK : (k + 4) * RANK, :])
        for j in range(4):
            turn_ref[pl.ds(k + j, 8, stride=RANK), :] = four[:, j * RANK : (j + 1) * RANK]
    pair_ref[...] = turn_ref[0 : 2 * RANK, :].astype(BF16)
    for copy in (sb_out, mom_out):
        copy.wait()


def pair_kernel(n_sums, own_ref, ra_ref, up_ref, out_hbm, block_ref, out_sems):
    odd = lax.rem(lax.axis_index("leaf"), 2)
    own = own_ref[...].astype(F32)
    other = ra_ref[BOX_AT:PAIR_ROWS, :].astype(F32)
    even_side = jnp.where(odd == 0, own, other)
    odd_side = jnp.where(odd == 0, other, own)
    both = own + other
    sums = [read_sum(both, j) for j in range(n_sums)]
    joined = jnp.concatenate([even_side[:, :RANK], odd_side[:, :RANK]], axis=1).astype(BF16)
    block = message(dot(joined, up_ref[...]).astype(BF16), sums)
    for c in range(COPIES):
        block_ref[c] = block
    outs = [
        pltpu.make_async_copy(block_ref, out_hbm.at[pl.ds(c * COPIES, COPIES)], out_sems.at[c])
        for c in range(CHIPS // COPIES)
    ]
    for out in outs:
        out.start()
    for out in outs:
        out.wait()


def turn_part(t, up_ref, couple_ref, nodes_ref, own_couple_ref, nodes_turn, couple_turn):
    position = lax.axis_index("leaf")
    pick = (lanes((DEVICES, NODES)) == rows((DEVICES, NODES)) + DEVICES).astype(F32).astype(BF16)
    own = one_hot(8, [level_start(level) + (position >> level) for level in range(LEVELS)])
    for k in range(0, TURN, 4):
        start = (t * TURN + k) * RANK
        turned = dot_nt(pick, up_ref[start : start + 4 * RANK, :])
        own_turned = dot_nt(own, couple_ref[start : start + 4 * RANK, :])
        for j in range(4):
            part = slice(j * RANK, (j + 1) * RANK)
            nodes_turn[pl.ds(k + j, DEVICES, stride=TURN), :] = turned[:, part]
            couple_turn[pl.ds(k + j, 8, stride=TURN), :] = own_turned[:, part]
    to = slice(t * TURN, (t + 1) * TURN)
    for n in range(DEVICES):
        nodes_ref[n, to, :] = nodes_turn[n * TURN : (n + 1) * TURN, :].astype(BF16)
    for n in range(8):
        own_couple_ref[n, to, :] = couple_turn[n * TURN : (n + 1) * TURN, :].astype(BF16)


def near_far_kernel(turn, near_index_ref, far_index_ref, *refs):
    sb_hbm, mom_hbm, ra_any, rb_any, tile_hbm, couple_ref, *refs = refs
    if turn:
        up_hbm, couple_t_hbm, near_hbm, far_hbm, nodes_hbm, own_couple_hbm, *refs = refs
    else:
        near_hbm, far_hbm, *refs = refs
    x_ref, mom_ref, ra_ref, rb_ref, left_ref, right_ref, tile_ref, *refs = refs
    near_ref, far_ref, in_sems, tile_sems, near_sems, far_sem, *refs = refs
    small = start_copies(
        (mom_hbm, rb_any, ra_any, sb_hbm),
        (mom_ref, rb_ref, ra_ref, x_ref.at[pl.ds(REACH, SLOTS)]),
        in_sems,
    )
    tiles = [
        pltpu.make_async_copy(tile_hbm.at[g], tile_ref.at[g], tile_sems.at[g])
        for g in range(SLOTS)
    ]
    for g in range(DEPTH):
        tiles[g].start()
    parts = []
    if turn:
        up_ref, couple_t_ref, nodes_ref, own_couple_ref, nodes_turn, couple_turn, *refs = refs
        turn_sems, turn_out_sems = refs
        chunk = TURN * RANK
        for t in range(RANK // TURN):
            part = pl.ds(t * chunk, chunk)
            parts.append(
                [
                    pltpu.make_async_copy(source.at[part], to.at[part], turn_sems.at[t, i])
                    for i, (source, to) in enumerate(
                        ((up_hbm, up_ref), (couple_t_hbm, couple_t_ref))
                    )
                ]
            )
    position = lax.axis_index("leaf")
    odd = lax.rem(position, 2)
    at = lanes()

    def spread_moments(source, first):
        for j in range(HALF):
            both = source[j * RHS : (j + 1) * RHS, :].astype(F32)
            turned = pltpu.roll(both, RANK, 1)
            low = at < RANK
            left_ref[first + 2 * j] = jnp.where(low, both, 0.0).astype(BF16)
            right_ref[first + 2 * j] = jnp.where(low, 0.0, turned).astype(BF16)
            left_ref[first + 2 * j + 1] = jnp.where(low, turned, 0.0).astype(BF16)
            right_ref[first + 2 * j + 1] = jnp.where(low, 0.0, both).astype(BF16)

    def edges(source, first):
        for j in range(REACH):
            for half in range(2):
                start = MOM_ROWS + (2 * j + half) * RHS
                x_ref[first + j, :, half * 128 : (half + 1) * 128] = source[start : start + RHS, :]

    small[0].wait()
    spread_moments(mom_ref, SLOTS)
    for copy in small[1:]:
        copy.wait()
    spread_moments(rb_ref, odd * (2 * SLOTS))
    spread_moments(ra_ref, (1 - odd) * (2 * SLOTS))
    edges(rb_ref, odd * (REACH + SLOTS))
    edges(ra_ref, (1 - odd) * (REACH + SLOTS))
    near_base = position * SLOTS - REACH
    far_base = position * SLOTS - SLOTS
    outs = []
    for g in range(SLOTS):
        if g + DEPTH < SLOTS:
            tiles[g + DEPTH].start()
        if turn and g % 4 == 0:
            for copy in parts[g // 4]:
                copy.start()
        tiles[g].wait()
        columns = [x_ref[near_index_ref[k, g] - near_base] for k in range(6)]
        near_ref[g] = dot(jnp.concatenate(columns, axis=1), tile_ref[g])
        out = pltpu.make_async_copy(near_ref.at[g], near_hbm.at[g], near_sems.at[g])
        out.start()
        outs.append(out)
        pairs = [
            left_ref[far_index_ref[2 * f, g] - far_base]
            + right_ref[far_index_ref[2 * f + 1, g] - far_base]
            for f in range(4)
        ]
        far_ref[:, g * RANK : (g + 1) * RANK] = dot(jnp.concatenate(pairs, axis=1), couple_ref[g])
        if turn and g % 4 == 3:
            t = g // 4
            for copy in parts[t]:
                copy.wait()
            turn_part(
                t, up_ref, couple_t_ref, nodes_ref, own_couple_ref, nodes_turn, couple_turn
            )
            to = pl.ds(t * TURN, TURN)
            for i, (source, target) in enumerate(
                ((nodes_ref, nodes_hbm), (own_couple_ref, own_couple_hbm))
            ):
                out = pltpu.make_async_copy(
                    source.at[:, to], target.at[:, to], turn_out_sems.at[t, i]
                )
                out.start()
                outs.append(out)
    out = pltpu.make_async_copy(far_ref, far_hbm, far_sem)
    out.start()
    outs.append(out)
    for out in outs:
        out.wait()


def tree_sweep(copies, ra_ref, gathered_ref, up_ref, pair_ref, couple_ref, nodes_ref):
    position = lax.axis_index("leaf")
    total = gathered_ref[0].astype(F32)
    for c in range(1, CHIPS):
        total = total + gathered_ref[c].astype(F32)
    current = [gathered_ref[c][:, :RANK] for c in range(CHIPS)]
    for level in range(1, LEVELS):
        if level == 2:
            copies[UP_PARTS - 1].wait()
        first = level_start(level) - DEVICES
        for n in range(len(current)):
            nodes_ref[first + n] = current[n]
        if level + 1 < LEVELS:
            following = []
            for m in range(len(current) // 2):
                start = (first + 2 * m) * RANK
                if level == 1 and 2 * m % UP_NODES == 0:
                    copies[2 * m // UP_NODES].wait()
                joined = jnp.concatenate([current[2 * m], current[2 * m + 1]], axis=1)
                following.append(dot(joined, up_ref[start : start + 2 * RANK, :]).astype(BF16))
            current = following
    copies[UP_PARTS].wait()
    sibling = ra_ref[BOX_AT:PAIR_ROWS, :][:, :RANK]
    locals_list = [dot(sibling, couple_ref[0:RANK, :])]
    for level in range(1, LEVELS):
        sibling = nodes_ref[level_start(level) - DEVICES + ((position >> level) ^ 1)]
        locals_list.append(dot(sibling, couple_ref[level * RANK : (level + 1) * RANK, :]))
    downward = locals_list[LEVELS - 1].astype(BF16)
    for level in reversed(range(LEVELS - 1)):
        if level == 0:
            up = pair_ref[pl.ds(pl.multiple_of(lax.rem(position, 2) * RANK, RANK), RANK), :]
        else:
            node = level_start(level) - DEVICES + (position >> level)
            up = up_ref[pl.ds(pl.multiple_of(node * RANK, RANK), RANK), :]
        downward = (locals_list[level] + dot_nt(downward, up)).astype(BF16)
    return downward, total


def spread_of(downward, far_ref, basis_ref, transfer_ref):
    block = block_of_lane()
    local_total = far_ref[...] + dot_nt(downward, transfer_ref[...])
    spread = []
    for q in range(SLOTS // 4):
        group = local_total[:, 4 * q * RANK : 4 * (q + 1) * RANK]
        apart = jnp.concatenate(
            [jnp.where(block == j, group, 0.0).astype(BF16) for j in range(4)], axis=0
        )
        four = dot(apart, basis_ref[4 * q * RANK : 4 * (q + 1) * RANK, :])
        spread += [four[j * RHS : (j + 1) * RHS, :] for j in range(4)]
    return spread


def start_tree(hbm, local, sems):
    up_hbm, up_ref = hbm[0], local[0]
    sizes = [UP_NODES] * (UP_PARTS - 1) + [CHIPS]
    cuts = [pl.ds(sum(sizes[:i]) * RANK, size * RANK) for i, size in enumerate(sizes)]
    sources = [up_hbm.at[cut] for cut in cuts] + list(hbm[1:])
    targets = [up_ref.at[cut] for cut in cuts] + list(local[1:])
    return start_copies(sources, targets, sems)


def middle_kernel(live_ref, ra_ref, gathered_ref, pair_ref, *refs):
    hbm, refs = refs[:7], refs[7:]
    pa_ref, pb_ref, own_ref, sb_hbm, mom_hbm, image_hbm, scal_hbm, *refs = refs
    local, refs = refs[:7], refs[7:]
    sb_ref, image_ref, scal_ref, nodes_ref, sems, out_sems, image_sems = refs
    copies = start_tree(hbm, local, sems)
    up_ref, couple_ref, near_ref, far_ref, transfer_ref, basis_ref, rh_ref = local
    downward, total = tree_sweep(
        copies, ra_ref, gathered_ref, up_ref, pair_ref, couple_ref, nodes_ref
    )
    for copy in copies[UP_PARTS + 1 :]:
        copy.wait()
    spread = spread_of(downward, far_ref, basis_ref, transfer_ref)
    outs = []
    square = read_sum(total, 0)
    norm = jnp.sqrt(square + EPSILON)
    scal_ref[...] = jnp.where(lanes() == 0, norm, square)
    inputs = []
    inner = jnp.zeros((RHS, POINTS), F32)
    length = jnp.zeros((RHS, POINTS), F32)
    for g in range(SLOTS):
        image = live_ref[g].astype(F32) * (near_ref[g] + spread[g]) / norm
        image_ref[g] = image
        if g % 4 == 3:
            four = pl.ds(g - 3, 4)
            out = pltpu.make_async_copy(
                image_ref.at[four], image_hbm.at[four], image_sems.at[g // 4]
            )
            out.start()
            outs.append(out)
        basis_one = rh_ref[g] * live_ref[g].astype(F32) / norm
        inner = inner + basis_one * image
        length = length + image * image
        sb = image.astype(BF16)
        sb_ref[g] = sb
        inputs.append(sb)
    outs += start_copies((sb_ref, scal_ref), (sb_hbm, scal_hbm), out_sems)
    moments, box = up_moments(inputs, basis_ref, transfer_ref)
    pack_out(inputs, moments, box, [row_sum(inner), row_sum(length)], pa_ref, pb_ref, own_ref)
    mom_out = pltpu.make_async_copy(pb_ref.at[pl.ds(0, MOM_ROWS)], mom_hbm, out_sems.at[2])
    mom_out.start()
    for out in (*outs, mom_out):
        out.wait()


def as_row(column, shift):
    return jnp.sum(jnp.where(lanes() == rows() + shift, column, 0.0), axis=0, keepdims=True)


def as_column(row, shift):
    return row_sum(jnp.where(lanes() == rows() + shift, row, 0.0))


def last_operator_kernel(live_ref, ra_ref, gathered_ref, pair_ref, *refs):
    hbm, refs = refs[:9], refs[9:]
    one_ref, two_ref, v_ref, send_ref, scal_ref, *refs = refs
    local, (nodes_ref, sems) = refs[:9], refs[9:]
    copies = start_tree(hbm, local, sems)
    up_ref, couple_ref, near_ref, far_ref, transfer_ref, basis_ref, rh_ref = local[:7]
    image_ref, scal_in_ref = local[7:]
    downward, total = tree_sweep(
        copies, ra_ref, gathered_ref, up_ref, pair_ref, couple_ref, nodes_ref
    )
    for copy in copies[UP_PARTS + 1 :]:
        copy.wait()
    spread = spread_of(downward, far_ref, basis_ref, transfer_ref)
    norm = scal_in_ref[:, 0:1]
    one_one = (scal_in_ref[:, 1:2] / norm) / norm
    first_inner = read_sum(total, 0)
    image_square = read_sum(total, 1)
    residue = image_square - 2.0 * first_inner * first_inner + first_inner * first_inner * one_one
    residue = jnp.maximum(residue, 0.0)
    first_length = jnp.sqrt(residue + EPSILON)
    one_two = (first_inner - first_inner * one_one) / first_length
    two_two = (residue / first_length) / first_length
    at = lanes()
    scal = jnp.zeros((RHS, 128), F32)
    for j, column in enumerate((norm, first_inner, first_length, one_one, one_two, two_two)):
        scal = jnp.where(at == j, column, scal)
    scal_ref[...] = scal
    cross = jnp.zeros((RHS, POINTS), F32)
    own = jnp.zeros((RHS, POINTS), F32)
    square = jnp.zeros((RHS, POINTS), F32)
    for g in range(SLOTS):
        image = image_ref[g]
        y = live_ref[g].astype(F32) * (near_ref[g] + spread[g])
        basis_one = rh_ref[g] * live_ref[g].astype(F32) / norm
        basis_two = (image - first_inner * basis_one) / first_length
        v = (y - first_inner * image) / first_length
        one_ref[g] = basis_one
        two_ref[g] = basis_two
        v_ref[g] = v
        cross = cross + basis_one * v
        own = own + basis_two * v
        square = square + v * v
    row = as_row(row_sum(cross), 0) + as_row(row_sum(own), 32) + as_row(row_sum(square), 64)
    for d in range(DEVICES):
        send_ref[d] = row


def final_kernel(one_ref, two_ref, v_ref, scal_ref, gathered_ref, next_ref, hess_ref):
    row = jnp.sum(gathered_ref[...], axis=0)
    cross, own, square = as_column(row, 0), as_column(row, 32), as_column(row, 64)
    norm, first_inner, first_length, one_one, one_two, two_two = (
        scal_ref[:, j : j + 1] for j in range(6)
    )
    residue = (
        square
        - 2.0 * cross * cross
        - 2.0 * own * own
        + cross * cross * one_one
        + own * own * two_two
        + 2.0 * cross * own * one_two
    )
    second_length = jnp.sqrt(jnp.maximum(residue, 0.0) + EPSILON)
    for j, column in enumerate((norm, first_inner, first_length, cross, own, second_length)):
        hess_ref[j : j + 1, :] = as_row(column, 0)[:, :RHS]
    for g in range(SLOTS):
        next_ref[g] = (v_ref[g] - cross * one_ref[g] - own * two_ref[g]) / second_length


def shape(dims, dtype):
    return jax.ShapeDtypeStruct(dims, dtype)


FIELD = (SLOTS, RHS, POINTS)
FAR_FIELD = (RHS, SLOTS * RANK)
PACKED = [shape((PAIR_ROWS, 128), BF16), shape((BOX_AT, 128), BF16), shape((RHS, 128), BF16)]
NODE_ROWS = DEVICES * RANK
BASIS = (SLOTS * RANK, POINTS)
TRANSFER = (SLOTS * RANK, RANK)
TURNED = (RANK * RANK, NODES)
GATHERED = (CHIPS, RHS, 128)
TREE_BUFFERS = [
    ((NODE_ROWS, RANK), BF16),
    ((8 * RANK, RANK), BF16),
    (FIELD, F32),
    (FAR_FIELD, F32),
    (TRANSFER, BF16),
    (BASIS, BF16),
    (FIELD, F32),
]
TREE_NODES = ((DEVICES - 2, RHS, RANK), BF16)
MIB = 1 << 20


def vmem(*kinds):
    return [pltpu.VMEM(*kind) for kind in kinds]


def sems(*dims):
    return [pltpu.SemaphoreType.DMA(dim) for dim in dims]


def in_hbm(*arrays):
    return [pltpu.with_memory_space_constraint(array, pltpu.HBM) for array in arrays]


def call(kernel, outs, in_specs, out_specs, scratch, mib, **more):
    return pl.pallas_call(
        kernel,
        out_shape=outs,
        in_specs=in_specs,
        out_specs=out_specs,
        scratch_shapes=scratch,
        compiler_params=pltpu.CompilerParams(vmem_limit_bytes=mib * MIB),
        **more,
    )


def on_device(
    right_hand,
    leaf_live,
    near_index,
    near_tile,
    far_index,
    far_couple,
    leaf_basis,
    leaf_transfer,
    tree_up,
    tree_couple,
):
    up_turned = tree_up.transpose(1, 2, 0).reshape(TURNED)
    couple_turned = tree_couple.transpose(1, 2, 0).reshape(TURNED)
    tiles = near_tile.reshape(SLOTS, 6 * POINTS, POINTS)
    couples = far_couple.reshape(SLOTS, 8 * RANK, RANK)
    indices = (near_index.T, far_index.T)
    leaf_basis = leaf_basis.reshape(BASIS)
    leaf_transfer = leaf_transfer.reshape(TRANSFER)
    same = [(i, i ^ 1) for i in range(DEVICES)]
    across = [(i, i + 1) for i in range(1, DEVICES - 1, 2)]
    across += [(j, i) for i, j in across]
    groups = [[2 * c + core for c in range(CHIPS)] for core in range(2)]

    def exchange(pa, pb, own, pair_up, n_sums):
        ra = lax.ppermute(pa, "leaf", same)
        rb = lax.ppermute(pb, "leaf", across)
        sent = call(
            functools.partial(pair_kernel, n_sums),
            pltpu.HBM(GATHERED, BF16),
            [VMEM, VMEM, VMEM],
            HBM,
            [*vmem(((COPIES, RHS, 128), BF16)), *sems((CHIPS // COPIES,))],
            4,
        )(own, ra, pair_up)
        gathered = lax.all_to_all(sent, "leaf", 0, 0, axis_index_groups=groups)
        return ra, rb, gathered

    def near_far(sb, mom, ra, rb, turn):
        outs = [pltpu.HBM(FIELD, F32), pltpu.HBM(FAR_FIELD, F32)]
        scratch = [
            *vmem(
                ((SLOTS + 2 * REACH, RHS, POINTS), BF16),
                ((MOM_ROWS, 128), BF16),
                ((PAIR_ROWS, 128), BF16),
                ((BOX_AT, 128), BF16),
                ((3 * SLOTS, RHS, 128), BF16),
                ((3 * SLOTS, RHS, 128), BF16),
                ((SLOTS, 6 * POINTS, POINTS), BF16),
                (FIELD, F32),
                (FAR_FIELD, F32),
            ),
            *sems((4,), (SLOTS,), (SLOTS,)),
            pltpu.SemaphoreType.DMA,
        ]
        more = []
        if turn:
            counts = (DEVICES, 8)
            outs += [pltpu.HBM((n, RANK, RANK), BF16) for n in counts]
            scratch += vmem(
                (TURNED, BF16),
                (TURNED, BF16),
                *(((n, RANK, RANK), BF16) for n in counts),
                *(((n * TURN, RANK), F32) for n in counts),
            )
            scratch += sems((RANK // TURN, 2), (RANK // TURN, 2))
            more = in_hbm(up_turned, couple_turned)
        return call(
            functools.partial(near_far_kernel, turn),
            outs,
            [SMEM, SMEM, HBM, HBM, ANY, ANY, HBM, VMEM, *([HBM] * len(more))],
            [HBM] * len(outs),
            scratch,
            40,
            cost_estimate=pl.CostEstimate(
                flops=1_000_000_000, bytes_accessed=16_000_000, transcendentals=0
            ),
        )(*indices, *in_hbm(sb, mom), ra, rb, *in_hbm(tiles), couples, *more)

    pa, pb, own, sb, mom, pair_up = call(
        first_kernel,
        [
            *PACKED,
            pltpu.HBM(FIELD, BF16),
            pltpu.HBM((MOM_ROWS, 128), BF16),
            shape((2 * RANK, RANK), BF16),
        ],
        [HBM] * 5,
        [VMEM] * 3 + [HBM] * 2 + [VMEM],
        [
            pltpu.SMEM((SLOTS,), jnp.int32),
            *vmem(
                (FIELD, F32),
                (BASIS, BF16),
                (TRANSFER, BF16),
                (TURNED, BF16),
                (FIELD, BF16),
                ((8 * RANK, RANK), F32),
            ),
            *sems((5,), (2,)),
        ],
        12,
    )(*in_hbm(leaf_live, right_hand, leaf_basis, leaf_transfer, up_turned))
    ra, rb, gathered = exchange(pa, pb, own, pair_up, 1)
    near, far, nodes, own_couple = near_far(sb, mom, ra, rb, True)
    up_nodes = nodes.reshape(NODE_ROWS, RANK)
    own_couple = own_couple.reshape(8 * RANK, RANK)
    count = len(TREE_BUFFERS)
    pa, pb, own, sb, mom, image, scal = call(
        middle_kernel,
        [
            *PACKED,
            pltpu.HBM(FIELD, BF16),
            pltpu.HBM((MOM_ROWS, 128), BF16),
            pltpu.HBM(FIELD, F32),
            pltpu.HBM((RHS, 128), F32),
        ],
        [SMEM, VMEM, VMEM, VMEM] + [HBM] * count,
        [VMEM] * 3 + [HBM] * 4,
        [
            *vmem(*TREE_BUFFERS, (FIELD, BF16), (FIELD, F32), ((RHS, 128), F32), TREE_NODES),
            *sems((count + UP_PARTS - 1,), (3,), (4,)),
        ],
        20,
    )(
        leaf_live, ra, gathered, pair_up,
        *in_hbm(up_nodes, own_couple, near, far, leaf_transfer, leaf_basis, right_hand),
    )
    ra, rb, gathered = exchange(pa, pb, own, pair_up, 2)
    near, far = near_far(sb, mom, ra, rb, False)
    one, two, v, sent, scal = call(
        last_operator_kernel,
        [shape(FIELD, F32)] * 3 + [shape((DEVICES, 1, 128), F32), shape((RHS, 128), F32)],
        [SMEM, VMEM, VMEM, VMEM] + [HBM] * (count + 2),
        [VMEM] * 5,
        [
            *vmem(*TREE_BUFFERS, (FIELD, F32), ((RHS, 128), F32), TREE_NODES),
            *sems((count + UP_PARTS + 1,)),
        ],
        20,
    )(
        leaf_live, ra, gathered, pair_up,
        *in_hbm(up_nodes, own_couple, near, far, leaf_transfer, leaf_basis, right_hand),
        *in_hbm(image, scal),
    )
    gathered = lax.all_to_all(sent, "leaf", 0, 0)
    return call(
        final_kernel, [shape(FIELD, F32), shape((6, RHS), F32)], [VMEM] * 5, [VMEM] * 2, [], 8
    )(one, two, v, scal, gathered)


def solution(mesh):
    placed = (
        P("leaf", None, None),
        P("leaf"),
        P("leaf", None),
        P("leaf", None, None, None),
        P("leaf", None),
        P("leaf", None, None, None),
        P("leaf", None, None),
        P("leaf", None, None),
        P(),
        P(),
    )
    return jax.shard_map(
        on_device,
        mesh=mesh,
        in_specs=placed,
        out_specs=(P("leaf", None, None), P()),
        check_vma=False,
    )
```

```python
import functools

import jax
import jax.numpy as jnp
from jax import lax
from jax.experimental import pallas as pl
from jax.experimental.pallas import tpu as pltpu
from jax.sharding import PartitionSpec as P


EPSILON = 1e-06
F32 = jnp.float32
BF16 = jnp.bfloat16
NT = (((1,), (1,)), ((), ()))

ANY = pl.BlockSpec(memory_space=pl.ANY)
VMEM = pl.BlockSpec(memory_space=pltpu.VMEM)
HBM = pl.BlockSpec(memory_space=pltpu.HBM)

SLOTS, RHS, POINTS, RANK = 16, 32, 256, 64
REACH = 2
HALF = SLOTS // 2
MOM_ROWS = HALF * RHS
NEAR_ROWS = REACH * 2 * RHS
BOX_AT = MOM_ROWS + NEAR_ROWS
PAIR_ROWS = BOX_AT + RHS
DEVICES = 128
LEVELS = 7
CHIPS = DEVICES // 2
NODES = 254
GROUPS = (4, 4, 4, 2, 2)
COPIES = 8


def dot(a, b):
    return jnp.dot(a, b, preferred_element_type=F32)


def dot_nt(a, b):
    return lax.dot_general(a, b, NT, preferred_element_type=F32)


def row_sum(x):
    return jnp.sum(x, axis=1, keepdims=True)


def lanes(shape=(RHS, 128)):
    return lax.broadcasted_iota(jnp.int32, shape, 1)


def rows(shape=(RHS, 128)):
    return lax.broadcasted_iota(jnp.int32, shape, 0)


def level_start(level):
    return 2 * DEVICES - 2 * (DEVICES >> level)


def three_parts(column):
    high = column.astype(BF16).astype(F32)
    rest = column - high
    middle = rest.astype(BF16).astype(F32)
    low = (rest - middle).astype(BF16).astype(F32)
    return high, middle, low


def sums_block(sums):
    at = lanes()
    block = jnp.zeros((RHS, 128), F32)
    for j, column in enumerate(sums):
        for k, part in enumerate(three_parts(column)):
            block = jnp.where(at == RANK + 3 * j + k, part, block)
    return block


def message(moment, sums):
    wide = jnp.concatenate([moment, jnp.zeros((RHS, 128 - RANK), F32)], axis=1)
    return jnp.where(lanes() < RANK, wide, sums_block(sums)).astype(BF16)


def read_sum(block, j):
    at = lanes()
    first = RANK + 3 * j
    return row_sum(jnp.where((at >= first) & (at < first + 3), block, 0.0))


def pack_out(inputs, moments, box, sums, pa_ref, pb_ref, own_ref):
    block = message(box, sums)
    own_ref[...] = block
    pa_ref[BOX_AT:PAIR_ROWS, :] = block
    for j in range(HALF):
        both = moments[:, j * 128 : (j + 1) * 128]
        pa_ref[j * RHS : (j + 1) * RHS, :] = both
        pb_ref[j * RHS : (j + 1) * RHS, :] = both
    odd = lax.rem(lax.axis_index("leaf"), 2)

    def edge(ref, first):
        for j in range(REACH):
            x = inputs[first + j]
            for half in range(2):
                start = MOM_ROWS + (2 * j + half) * RHS
                ref[start : start + RHS, :] = x[:, half * 128 : (half + 1) * 128]

    @pl.when(odd == 0)
    def _():
        edge(pa_ref, SLOTS - REACH)
        edge(pb_ref, 0)

    @pl.when(odd == 1)
    def _():
        edge(pa_ref, 0)
        edge(pb_ref, SLOTS - REACH)


def block_of_lane():
    return lanes((RHS, 4 * RANK)) // RANK


def up_moments(inputs, basis_ref, transfer_ref):
    block = block_of_lane()
    groups = []
    for q in range(SLOTS // 4):
        four = jnp.concatenate(inputs[4 * q : 4 * q + 4], axis=0)
        crossed = dot_nt(four, basis_ref[4 * q * RANK : 4 * (q + 1) * RANK, :])
        group = crossed[0:RHS, :]
        for j in range(1, 4):
            group = jnp.where(block == j, crossed[j * RHS : (j + 1) * RHS, :], group)
        groups.append(group.astype(BF16))
    moments = jnp.concatenate(groups, axis=1)
    return moments, dot(moments, transfer_ref[...])


def start_copies(sources, targets, sems):
    copies = [
        pltpu.make_async_copy(source, target, sems.at[i])
        for i, (source, target) in enumerate(zip(sources, targets, strict=True))
    ]
    for copy in copies:
        copy.start()
    return copies


def one_hot(count, nodes):
    at, row = lanes((count, NODES)), rows((count, NODES))
    block = jnp.zeros((count, NODES), F32)
    for i, node in enumerate(nodes):
        block = jnp.where((row == i) & (at == node), 1.0, block)
    return block.astype(BF16)


def pick_nodes(nodes, turned_ref, out_ref, rows_ref):
    pick = one_hot(8, nodes)
    for k in range(0, RANK, 4):
        four = dot_nt(pick, turned_ref[k * RANK : (k + 4) * RANK, :])
        for j in range(4):
            rows_ref[pl.ds(k + j, 8, stride=RANK), :] = four[:, j * RANK : (j + 1) * RANK]
    out_ref[...] = rows_ref[...].astype(BF16)


def first_kernel(
    live_hbm,
    rh_hbm,
    basis_hbm,
    transfer_hbm,
    up_hbm,
    couple_hbm,
    pa_ref,
    pb_ref,
    own_ref,
    sb_hbm,
    mom_hbm,
    pair_ref,
    couple_zero_ref,
    out_path_ref,
    down_path_ref,
    live_ref,
    rh_ref,
    basis_ref,
    transfer_ref,
    up_ref,
    couple_ref,
    sb_ref,
    up_nodes_ref,
    couple_nodes_ref,
    up_rows_ref,
    couple_rows_ref,
    sems,
    out_sems,
):
    up_in, couple_in, *copies = start_copies(
        (up_hbm, couple_hbm, live_hbm, rh_hbm, basis_hbm, transfer_hbm),
        (up_ref, couple_ref, live_ref, rh_ref, basis_ref, transfer_ref),
        sems,
    )
    position = lax.axis_index("leaf")
    odd = lax.rem(position, 2)
    path = [level_start(level) + (position >> level) for level in range(1, LEVELS - 1)]
    beside = [level_start(level) + ((position >> level) ^ 1) for level in range(1, LEVELS)]
    up_in.wait()
    pick_nodes((position - odd, position - odd + 1, *path), up_ref, up_nodes_ref, up_rows_ref)
    couple_in.wait()
    pick_nodes((position, *beside), couple_ref, couple_nodes_ref, couple_rows_ref)
    for copy in copies:
        copy.wait()
    inputs = []
    square = jnp.zeros((RHS, POINTS), F32)
    for g in range(SLOTS):
        s = rh_ref[g] * live_ref[g].astype(F32)
        square = square + s * s
        sb = s.astype(BF16)
        sb_ref[g] = sb
        inputs.append(sb)
    sb_out = pltpu.make_async_copy(sb_ref, sb_hbm, out_sems.at[0])
    sb_out.start()
    moments, box = up_moments(inputs, basis_ref, transfer_ref)
    pack_out(inputs, moments, box, [row_sum(square)], pa_ref, pb_ref, own_ref)
    mom_out = pltpu.make_async_copy(pb_ref.at[pl.ds(0, MOM_ROWS)], mom_hbm, out_sems.at[1])
    mom_out.start()
    pair_ref[...] = up_nodes_ref[0 : 2 * RANK, :]
    couple_zero_ref[...] = couple_nodes_ref[0:RANK, :]

    def node(ref, i):
        return ref[i * RANK : (i + 1) * RANK, :]

    up_zero = up_nodes_ref[pl.ds(pl.multiple_of(odd * RANK, RANK), RANK), :]
    chain = None
    outward = []
    for level in range(1, LEVELS):
        to = slice((level - 1) * RANK, level * RANK)
        if chain is None:
            outward.append(node(couple_nodes_ref, level).astype(F32))
            down_path_ref[to, :] = up_zero
            chain = node(up_nodes_ref, 2)
        else:
            outward.append(dot(chain, node(couple_nodes_ref, level)))
            down_path_ref[to, :] = dot(up_zero, chain).astype(BF16)
            if level + 1 < LEVELS:
                chain = dot(chain, node(up_nodes_ref, level + 1)).astype(BF16)
    out_path_ref[...] = jnp.concatenate(outward, axis=1).astype(BF16)
    for copy in (sb_out, mom_out):
        copy.wait()


def pair_kernel(n_sums, own_ref, ra_ref, up_ref, path_ref, out_hbm, block_ref, out_sems):
    position = lax.axis_index("leaf")
    odd = lax.rem(position, 2)
    chip = position >> 1
    own = own_ref[...].astype(F32)
    other = ra_ref[BOX_AT:PAIR_ROWS, :].astype(F32)
    even_side = jnp.where(odd == 0, own, other)
    odd_side = jnp.where(odd == 0, other, own)
    both = own + other
    joined = jnp.concatenate([even_side[:, :RANK], odd_side[:, :RANK]], axis=1).astype(BF16)
    moment = dot(joined, up_ref[...]).astype(BF16)
    levels = dot(moment, path_ref[...])
    sums = sums_block([read_sum(both, j) for j in range(n_sums)])
    low = lanes() < RANK
    outs = []
    at = 0
    for level in range(LEVELS):
        count = 1 if level == 0 else 1 << (level - 1)
        if level == 0:
            block, first = sums, chip
        else:
            group = levels[:, (level - 1) // 2 * 128 : (level + 1) // 2 * 128]
            if level % 2 == 0:
                group = pltpu.roll(group, RANK, 1)
            block = jnp.where(low, group, sums)
            first = ((chip >> (level - 1)) ^ 1) << (level - 1)
        block = block.astype(BF16)
        copies = min(count, COPIES)
        for c in range(copies):
            block_ref[at + c] = block
        for i in range(count // copies):
            out = pltpu.make_async_copy(
                block_ref.at[pl.ds(at, copies)],
                out_hbm.at[pl.ds(first + i * copies, copies)],
                out_sems.at[len(outs)],
            )
            out.start()
            outs.append(out)
        at += copies
    for out in outs:
        out.wait()


def near_far_kernel(
    near_index_hbm,
    far_index_hbm,
    sb_hbm,
    mom_hbm,
    ra_any,
    rb_any,
    tile_hbm,
    couple_ref,
    near_hbm,
    far_ref,
    near_index_ref,
    far_index_ref,
    near_ref,
    x_ref,
    mom_ref,
    ra_ref,
    rb_ref,
    left_ref,
    right_ref,
    tile_ref,
    in_sems,
    tile_sems,
    near_sems,
):
    small = start_copies(
        (mom_hbm, rb_any, ra_any, sb_hbm, near_index_hbm, far_index_hbm),
        (
            mom_ref,
            rb_ref,
            ra_ref,
            x_ref.at[pl.ds(REACH, SLOTS)],
            near_index_ref,
            far_index_ref,
        ),
        in_sems,
    )
    parts = [pl.ds(sum(GROUPS[:i]), size) for i, size in enumerate(GROUPS)]
    tiles = start_copies(
        [tile_hbm.at[part] for part in parts], [tile_ref.at[part] for part in parts], tile_sems
    )
    position = lax.axis_index("leaf")
    odd = lax.rem(position, 2)
    low = lanes() < RANK

    def spread_moments(source, first):
        for j in range(HALF):
            both = source[j * RHS : (j + 1) * RHS, :].astype(F32)
            turned = pltpu.roll(both, RANK, 1)
            left_ref[first + 2 * j] = jnp.where(low, both, 0.0).astype(BF16)
            right_ref[first + 2 * j] = jnp.where(low, 0.0, turned).astype(BF16)
            left_ref[first + 2 * j + 1] = jnp.where(low, turned, 0.0).astype(BF16)
            right_ref[first + 2 * j + 1] = jnp.where(low, 0.0, both).astype(BF16)

    def edges(source, first):
        for j in range(REACH):
            for half in range(2):
                start = MOM_ROWS + (2 * j + half) * RHS
                x_ref[first + j, :, half * 128 : (half + 1) * 128] = source[start : start + RHS, :]

    for copy in small:
        copy.wait()
    spread_moments(mom_ref, SLOTS)
    spread_moments(rb_ref, odd * (2 * SLOTS))
    spread_moments(ra_ref, (1 - odd) * (2 * SLOTS))
    edges(rb_ref, odd * (REACH + SLOTS))
    edges(ra_ref, (1 - odd) * (REACH + SLOTS))
    near_base = position * SLOTS - REACH
    far_base = position * SLOTS - SLOTS
    for g in range(SLOTS):
        pairs = [
            left_ref[far_index_ref[2 * f, g] - far_base]
            + right_ref[far_index_ref[2 * f + 1, g] - far_base]
            for f in range(4)
        ]
        far_ref[:, g * RANK : (g + 1) * RANK] = dot(jnp.concatenate(pairs, axis=1), couple_ref[g])
    outs = []
    for i, part in enumerate(parts):
        tiles[i].wait()
        for g in range(part.start, part.start + part.size):
            columns = [x_ref[near_index_ref[k, g] - near_base] for k in range(6)]
            near_ref[g] = dot(jnp.concatenate(columns, axis=1), tile_ref[g])
        out = pltpu.make_async_copy(near_ref.at[part], near_hbm.at[part], near_sems.at[i])
        out.start()
        outs.append(out)
    for out in outs:
        out.wait()


def tree_sweep(ra_ref, gathered_ref, couple_zero_ref, down_path_ref):
    chip = lax.axis_index("leaf") >> 1
    total = gathered_ref[chip].astype(F32)
    sibling = ra_ref[BOX_AT:PAIR_ROWS, :][:, :RANK]
    downward = dot(sibling, couple_zero_ref[...])
    for level in range(1, LEVELS):
        level_sum = jnp.zeros((RHS, 128), F32)
        for x in range(1 << (level - 1), 1 << level):
            level_sum = level_sum + gathered_ref[chip ^ x].astype(F32)
        total = total + level_sum
        path = down_path_ref[(level - 1) * RANK : level * RANK, :]
        downward = downward + dot_nt(level_sum[:, :RANK].astype(BF16), path)
    return downward.astype(BF16), total


def spread_of(downward, far_ref, basis_ref, transfer_ref):
    block = block_of_lane()
    local_total = far_ref[...] + dot_nt(downward, transfer_ref[...])
    spread = []
    for q in range(SLOTS // 4):
        group = local_total[:, 4 * q * RANK : 4 * (q + 1) * RANK]
        apart = jnp.concatenate(
            [jnp.where(block == j, group, 0.0).astype(BF16) for j in range(4)], axis=0
        )
        four = dot(apart, basis_ref[4 * q * RANK : 4 * (q + 1) * RANK, :])
        spread += [four[j * RHS : (j + 1) * RHS, :] for j in range(4)]
    return spread


def middle_kernel(
    ra_ref,
    gathered_ref,
    couple_zero_ref,
    down_path_ref,
    far_ref,
    *refs,
):
    hbm, refs = refs[:5], refs[5:]
    pa_ref, pb_ref, own_ref, scal_ref, sb_hbm, mom_hbm, image_hbm, *refs = refs
    local, refs = refs[:5], refs[5:]
    sb_ref, image_ref, sems, out_sems, image_sems = refs
    copies = start_copies(hbm, local, sems)
    live_ref, transfer_ref, basis_ref, near_ref, rh_ref = local
    downward, total = tree_sweep(ra_ref, gathered_ref, couple_zero_ref, down_path_ref)
    for copy in copies:
        copy.wait()
    spread = spread_of(downward, far_ref, basis_ref, transfer_ref)
    outs = []
    square = read_sum(total, 0)
    norm = jnp.sqrt(square + EPSILON)
    scal_ref[...] = jnp.where(lanes() == 0, norm, square)
    inputs = []
    inner = jnp.zeros((RHS, POINTS), F32)
    length = jnp.zeros((RHS, POINTS), F32)
    for g in range(SLOTS):
        image = live_ref[g].astype(F32) * (near_ref[g] + spread[g]) / norm
        image_ref[g] = image
        if g % 4 == 3:
            four = pl.ds(g - 3, 4)
            out = pltpu.make_async_copy(
                image_ref.at[four], image_hbm.at[four], image_sems.at[g // 4]
            )
            out.start()
            outs.append(out)
        basis_one = rh_ref[g] * live_ref[g].astype(F32) / norm
        inner = inner + basis_one * image
        length = length + image * image
        sb = image.astype(BF16)
        sb_ref[g] = sb
        inputs.append(sb)
    outs += start_copies((sb_ref,), (sb_hbm,), out_sems)
    moments, box = up_moments(inputs, basis_ref, transfer_ref)
    pack_out(inputs, moments, box, [row_sum(inner), row_sum(length)], pa_ref, pb_ref, own_ref)
    mom_out = pltpu.make_async_copy(pb_ref.at[pl.ds(0, MOM_ROWS)], mom_hbm, out_sems.at[1])
    mom_out.start()
    for out in (*outs, mom_out):
        out.wait()


def as_row(column, shift):
    return jnp.sum(jnp.where(lanes() == rows() + shift, column, 0.0), axis=0, keepdims=True)


def as_column(row, shift):
    return row_sum(jnp.where(lanes() == rows() + shift, row, 0.0))


def last_operator_kernel(
    ra_ref,
    gathered_ref,
    couple_zero_ref,
    down_path_ref,
    scal_in_ref,
    far_ref,
    *refs,
):
    hbm, refs = refs[:6], refs[6:]
    one_ref, two_ref, v_ref, send_ref, scal_ref, *refs = refs
    local, (sems,) = refs[:6], refs[6:]
    copies = start_copies(hbm, local, sems)
    live_ref, transfer_ref, basis_ref, near_ref, rh_ref, image_ref = local
    downward, total = tree_sweep(ra_ref, gathered_ref, couple_zero_ref, down_path_ref)
    for copy in copies:
        copy.wait()
    spread = spread_of(downward, far_ref, basis_ref, transfer_ref)
    norm = scal_in_ref[:, 0:1]
    one_one = (scal_in_ref[:, 1:2] / norm) / norm
    first_inner = read_sum(total, 0)
    image_square = read_sum(total, 1)
    residue = image_square - 2.0 * first_inner * first_inner + first_inner * first_inner * one_one
    residue = jnp.maximum(residue, 0.0)
    first_length = jnp.sqrt(residue + EPSILON)
    one_two = (first_inner - first_inner * one_one) / first_length
    two_two = (residue / first_length) / first_length
    at = lanes()
    scal = jnp.zeros((RHS, 128), F32)
    for j, column in enumerate((norm, first_inner, first_length, one_one, one_two, two_two)):
        scal = jnp.where(at == j, column, scal)
    scal_ref[...] = scal
    cross = jnp.zeros((RHS, POINTS), F32)
    own = jnp.zeros((RHS, POINTS), F32)
    square = jnp.zeros((RHS, POINTS), F32)
    for g in range(SLOTS):
        image = image_ref[g]
        y = live_ref[g].astype(F32) * (near_ref[g] + spread[g])
        basis_one = rh_ref[g] * live_ref[g].astype(F32) / norm
        basis_two = (image - first_inner * basis_one) / first_length
        v = (y - first_inner * image) / first_length
        one_ref[g] = basis_one
        two_ref[g] = basis_two
        v_ref[g] = v
        cross = cross + basis_one * v
        own = own + basis_two * v
        square = square + v * v
    row = as_row(row_sum(cross), 0) + as_row(row_sum(own), 32) + as_row(row_sum(square), 64)
    for d in range(DEVICES):
        send_ref[d] = row


def final_kernel(one_ref, two_ref, v_ref, scal_ref, gathered_ref, next_ref, hess_ref):
    row = jnp.sum(gathered_ref[...], axis=0)
    cross, own, square = as_column(row, 0), as_column(row, 32), as_column(row, 64)
    norm, first_inner, first_length, one_one, one_two, two_two = (
        scal_ref[:, j : j + 1] for j in range(6)
    )
    residue = (
        square
        - 2.0 * cross * cross
        - 2.0 * own * own
        + cross * cross * one_one
        + own * own * two_two
        + 2.0 * cross * own * one_two
    )
    second_length = jnp.sqrt(jnp.maximum(residue, 0.0) + EPSILON)
    for j, column in enumerate((norm, first_inner, first_length, cross, own, second_length)):
        hess_ref[j : j + 1, :] = as_row(column, 0)[:, :RHS]
    for g in range(SLOTS):
        next_ref[g] = (v_ref[g] - cross * one_ref[g] - own * two_ref[g]) / second_length


def shape(dims, dtype):
    return jax.ShapeDtypeStruct(dims, dtype)


FIELD = (SLOTS, RHS, POINTS)
FAR_FIELD = (RHS, SLOTS * RANK)
PACKED = [shape((PAIR_ROWS, 128), BF16), shape((BOX_AT, 128), BF16), shape((RHS, 128), BF16)]
BASIS = (SLOTS * RANK, POINTS)
TRANSFER = (SLOTS * RANK, RANK)
TURNED = (RANK * RANK, NODES)
GATHERED = (CHIPS, RHS, 128)
LEAF_BUFFERS = [(TRANSFER, BF16), (BASIS, BF16), (FIELD, F32), (FIELD, F32)]
PATH = (LEVELS - 1) * RANK
WEIGHTS = [
    shape((2 * RANK, RANK), BF16),
    shape((RANK, RANK), BF16),
    shape((RANK, PATH), BF16),
    shape((PATH, RANK), BF16),
]
MIB = 1 << 20


def vmem(*kinds):
    return [pltpu.VMEM(*kind) for kind in kinds]


def sems(*dims):
    return [pltpu.SemaphoreType.DMA(dim) for dim in dims]


def in_hbm(*arrays):
    return [pltpu.with_memory_space_constraint(array, pltpu.HBM) for array in arrays]


def call(kernel, outs, in_specs, out_specs, scratch, mib, **more):
    return pl.pallas_call(
        kernel,
        out_shape=outs,
        in_specs=in_specs,
        out_specs=out_specs,
        scratch_shapes=scratch,
        compiler_params=pltpu.CompilerParams(vmem_limit_bytes=mib * MIB),
        **more,
    )


def on_device(
    right_hand,
    leaf_live,
    near_index,
    near_tile,
    far_index,
    far_couple,
    leaf_basis,
    leaf_transfer,
    tree_up,
    tree_couple,
):
    up_turned = tree_up.transpose(1, 2, 0).reshape(TURNED)
    couple_turned = tree_couple.transpose(1, 2, 0).reshape(TURNED)
    tiles = near_tile.reshape(SLOTS, 6 * POINTS, POINTS)
    couples = far_couple.reshape(SLOTS, 8 * RANK, RANK)
    indices = (near_index.T, far_index.T)
    leaf_basis = leaf_basis.reshape(BASIS)
    leaf_transfer = leaf_transfer.reshape(TRANSFER)
    same = [(i, i ^ 1) for i in range(DEVICES)]
    across = [(i, i + 1) for i in range(1, DEVICES - 1, 2)]
    across += [(j, i) for i, j in across]
    groups = [[2 * c + core for c in range(CHIPS)] for core in range(2)]

    def exchange(pa, pb, own, pair_up, out_path, n_sums):
        ra = lax.ppermute(pa, "leaf", same)
        rb = lax.ppermute(pb, "leaf", across)
        sent = call(
            functools.partial(pair_kernel, n_sums),
            pltpu.HBM(GATHERED, BF16),
            [VMEM] * 4,
            HBM,
            [*vmem(((4 * COPIES, RHS, 128), BF16)), *sems((11,))],
            4,
        )(own, ra, pair_up, out_path)
        gathered = lax.all_to_all(sent, "leaf", 0, 0, axis_index_groups=groups)
        return ra, rb, gathered

    def near_far(sb, mom, ra, rb):
        return call(
            near_far_kernel,
            [pltpu.HBM(FIELD, F32), shape(FAR_FIELD, F32)],
            [HBM, HBM, HBM, HBM, ANY, ANY, HBM, VMEM],
            [HBM, VMEM],
            [
                pltpu.SMEM((6, SLOTS), jnp.int32),
                pltpu.SMEM((8, SLOTS), jnp.int32),
                *vmem(
                    (FIELD, F32),
                    ((SLOTS + 2 * REACH, RHS, POINTS), BF16),
                    ((MOM_ROWS, 128), BF16),
                    ((PAIR_ROWS, 128), BF16),
                    ((BOX_AT, 128), BF16),
                    ((3 * SLOTS, RHS, 128), BF16),
                    ((3 * SLOTS, RHS, 128), BF16),
                    ((SLOTS, 6 * POINTS, POINTS), BF16),
                ),
                *sems((6,), (len(GROUPS),), (len(GROUPS),)),
            ],
            40,
            cost_estimate=pl.CostEstimate(
                flops=1_000_000_000, bytes_accessed=16_000_000, transcendentals=0
            ),
        )(*in_hbm(*indices, sb, mom), ra, rb, *in_hbm(tiles), couples)

    pa, pb, own, sb, mom, pair_up, couple_zero, out_path, down_path = call(
        first_kernel,
        [*PACKED, pltpu.HBM(FIELD, BF16), pltpu.HBM((MOM_ROWS, 128), BF16), *WEIGHTS],
        [HBM] * 6,
        [VMEM] * 3 + [HBM] * 2 + [VMEM] * 4,
        [
            pltpu.SMEM((SLOTS,), jnp.int32),
            *vmem(
                (FIELD, F32),
                (BASIS, BF16),
                (TRANSFER, BF16),
                (TURNED, BF16),
                (TURNED, BF16),
                (FIELD, BF16),
                ((8 * RANK, RANK), BF16),
                ((8 * RANK, RANK), BF16),
                ((8 * RANK, RANK), F32),
                ((8 * RANK, RANK), F32),
            ),
            *sems((6,), (2,)),
        ],
        16,
    )(*in_hbm(leaf_live, right_hand, leaf_basis, leaf_transfer, up_turned, couple_turned))
    ra, rb, gathered = exchange(pa, pb, own, pair_up, out_path, 1)
    near, far = near_far(sb, mom, ra, rb)
    count = len(LEAF_BUFFERS)
    pa, pb, own, scal, sb, mom, image = call(
        middle_kernel,
        [
            *PACKED,
            shape((RHS, 128), F32),
            pltpu.HBM(FIELD, BF16),
            pltpu.HBM((MOM_ROWS, 128), BF16),
            pltpu.HBM(FIELD, F32),
        ],
        [VMEM] * 5 + [HBM] * (count + 1),
        [VMEM] * 4 + [HBM] * 3,
        [
            pltpu.SMEM((SLOTS,), jnp.int32),
            *vmem(*LEAF_BUFFERS, (FIELD, BF16), (FIELD, F32)),
            *sems((count + 1,), (2,), (4,)),
        ],
        16,
    )(
        ra, gathered, couple_zero, down_path, far,
        *in_hbm(leaf_live, leaf_transfer, leaf_basis, near, right_hand),
    )
    ra, rb, gathered = exchange(pa, pb, own, pair_up, out_path, 2)
    near, far = near_far(sb, mom, ra, rb)
    one, two, v, sent, scal = call(
        last_operator_kernel,
        [shape(FIELD, F32)] * 3 + [shape((DEVICES, 1, 128), F32), shape((RHS, 128), F32)],
        [VMEM] * 6 + [HBM] * (count + 2),
        [VMEM] * 5,
        [
            pltpu.SMEM((SLOTS,), jnp.int32),
            *vmem(*LEAF_BUFFERS, (FIELD, F32)),
            *sems((count + 2,)),
        ],
        16,
    )(
        ra, gathered, couple_zero, down_path, scal, far,
        *in_hbm(leaf_live, leaf_transfer, leaf_basis, near, right_hand, image),
    )
    gathered = lax.all_to_all(sent, "leaf", 0, 0)
    return call(
        final_kernel, [shape(FIELD, F32), shape((6, RHS), F32)], [VMEM] * 5, [VMEM] * 2, [], 8
    )(one, two, v, scal, gathered)


def solution(mesh):
    placed = (
        P("leaf", None, None),
        P("leaf"),
        P("leaf", None),
        P("leaf", None, None, None),
        P("leaf", None),
        P("leaf", None, None, None),
        P("leaf", None, None),
        P("leaf", None, None),
        P(),
        P(),
    )
    return jax.shard_map(
        on_device,
        mesh=mesh,
        in_specs=placed,
        out_specs=(P("leaf", None, None), P()),
        check_vma=False,
    )
```

```python
import functools

import jax
import jax.numpy as jnp
from jax import lax
from jax.experimental import pallas as pl
from jax.experimental.pallas import tpu as pltpu
from jax.sharding import PartitionSpec as P


EPSILON = 1e-06
F32 = jnp.float32
BF16 = jnp.bfloat16
NT = (((1,), (1,)), ((), ()))

ANY = pl.BlockSpec(memory_space=pl.ANY)
VMEM = pl.BlockSpec(memory_space=pltpu.VMEM)
HBM = pl.BlockSpec(memory_space=pltpu.HBM)

SLOTS, RHS, POINTS, RANK = 16, 32, 256, 64
REACH = 2
HALF = SLOTS // 2
MOM_ROWS = HALF * RHS
NEAR_ROWS = REACH * 2 * RHS
BOX_AT = MOM_ROWS + NEAR_ROWS
PAIR_ROWS = BOX_AT + RHS
DEVICES = 128
LEVELS = 7
CHIPS = DEVICES // 2
NODES = 254
GROUPS = (4, 4, 4, 2, 2)
COPIES = 8


def dot(a, b):
    return jnp.dot(a, b, preferred_element_type=F32)


def dot_nt(a, b):
    return lax.dot_general(a, b, NT, preferred_element_type=F32)


def row_sum(x):
    return jnp.sum(x, axis=1, keepdims=True)


def lanes(shape=(RHS, 128)):
    return lax.broadcasted_iota(jnp.int32, shape, 1)


def rows(shape=(RHS, 128)):
    return lax.broadcasted_iota(jnp.int32, shape, 0)


def level_start(level):
    return 2 * DEVICES - 2 * (DEVICES >> level)


def three_parts(column):
    high = column.astype(BF16).astype(F32)
    rest = column - high
    middle = rest.astype(BF16).astype(F32)
    low = (rest - middle).astype(BF16).astype(F32)
    return high, middle, low


def sums_block(sums):
    at = lanes()
    block = jnp.zeros((RHS, 128), F32)
    for j, column in enumerate(sums):
        for k, part in enumerate(three_parts(column)):
            block = jnp.where(at == RANK + 3 * j + k, part, block)
    return block


def message(moment, sums):
    wide = jnp.concatenate([moment, jnp.zeros((RHS, 128 - RANK), F32)], axis=1)
    return jnp.where(lanes() < RANK, wide, sums_block(sums)).astype(BF16)


def read_sum(block, j):
    at = lanes()
    first = RANK + 3 * j
    return row_sum(jnp.where((at >= first) & (at < first + 3), block, 0.0))


def pack_out(inputs, moments, box, sums, pa_ref, pb_ref, own_ref):
    block = message(box, sums)
    own_ref[...] = block
    pa_ref[BOX_AT:PAIR_ROWS, :] = block
    for j in range(HALF):
        both = moments[:, j * 128 : (j + 1) * 128]
        pa_ref[j * RHS : (j + 1) * RHS, :] = both
        pb_ref[j * RHS : (j + 1) * RHS, :] = both
    odd = lax.rem(lax.axis_index("leaf"), 2)

    def edge(ref, first):
        for j in range(REACH):
            x = inputs[first + j]
            for half in range(2):
                start = MOM_ROWS + (2 * j + half) * RHS
                ref[start : start + RHS, :] = x[:, half * 128 : (half + 1) * 128]

    @pl.when(odd == 0)
    def _():
        edge(pa_ref, SLOTS - REACH)
        edge(pb_ref, 0)

    @pl.when(odd == 1)
    def _():
        edge(pa_ref, 0)
        edge(pb_ref, SLOTS - REACH)


def block_of_lane():
    return lanes((RHS, 4 * RANK)) // RANK


def up_moments(inputs, basis_ref, transfer_ref):
    block = block_of_lane()
    groups = []
    for q in range(SLOTS // 4):
        four = jnp.concatenate(inputs[4 * q : 4 * q + 4], axis=0)
        crossed = dot_nt(four, basis_ref[4 * q * RANK : 4 * (q + 1) * RANK, :])
        group = crossed[0:RHS, :]
        for j in range(1, 4):
            group = jnp.where(block == j, crossed[j * RHS : (j + 1) * RHS, :], group)
        groups.append(group.astype(BF16))
    moments = jnp.concatenate(groups, axis=1)
    return moments, dot(moments, transfer_ref[...])


def start_copies(sources, targets, sems):
    copies = [
        pltpu.make_async_copy(source, target, sems.at[i])
        for i, (source, target) in enumerate(zip(sources, targets, strict=True))
    ]
    for copy in copies:
        copy.start()
    return copies


def one_hot(count, nodes):
    at, row = lanes((count, NODES)), rows((count, NODES))
    block = jnp.zeros((count, NODES), F32)
    for i, node in enumerate(nodes):
        block = jnp.where((row == i) & (at == node), 1.0, block)
    return block.astype(BF16)


def pick_nodes(nodes, turned_ref, out_ref, rows_ref):
    pick = one_hot(8, nodes)
    for k in range(0, RANK, 4):
        four = dot_nt(pick, turned_ref[k * RANK : (k + 4) * RANK, :])
        for j in range(4):
            rows_ref[pl.ds(k + j, 8, stride=RANK), :] = four[:, j * RANK : (j + 1) * RANK]
    out_ref[...] = rows_ref[...].astype(BF16)


def first_kernel(
    live_hbm,
    rh_hbm,
    basis_hbm,
    transfer_hbm,
    up_hbm,
    couple_hbm,
    pa_ref,
    pb_ref,
    own_ref,
    sb_hbm,
    pair_ref,
    couple_zero_ref,
    out_path_ref,
    down_path_ref,
    live_ref,
    rh_ref,
    basis_ref,
    transfer_ref,
    up_ref,
    couple_ref,
    sb_ref,
    up_nodes_ref,
    couple_nodes_ref,
    up_rows_ref,
    couple_rows_ref,
    sems,
    out_sem,
):
    up_in, couple_in, *copies = start_copies(
        (up_hbm, couple_hbm, live_hbm, rh_hbm, basis_hbm, transfer_hbm),
        (up_ref, couple_ref, live_ref, rh_ref, basis_ref, transfer_ref),
        sems,
    )
    position = lax.axis_index("leaf")
    odd = lax.rem(position, 2)
    path = [level_start(level) + (position >> level) for level in range(1, LEVELS - 1)]
    beside = [level_start(level) + ((position >> level) ^ 1) for level in range(1, LEVELS)]
    up_in.wait()
    pick_nodes((position - odd, position - odd + 1, *path), up_ref, up_nodes_ref, up_rows_ref)
    couple_in.wait()
    pick_nodes((position, *beside), couple_ref, couple_nodes_ref, couple_rows_ref)
    for copy in copies:
        copy.wait()
    inputs = []
    square = jnp.zeros((RHS, POINTS), F32)
    for g in range(SLOTS):
        s = rh_ref[g] * live_ref[g].astype(F32)
        square = square + s * s
        sb = s.astype(BF16)
        sb_ref[g] = sb
        inputs.append(sb)
    sb_out = pltpu.make_async_copy(sb_ref, sb_hbm, out_sem)
    sb_out.start()
    moments, box = up_moments(inputs, basis_ref, transfer_ref)
    pack_out(inputs, moments, box, [row_sum(square)], pa_ref, pb_ref, own_ref)
    pair_ref[...] = up_nodes_ref[0 : 2 * RANK, :]
    couple_zero_ref[...] = couple_nodes_ref[0:RANK, :]

    def node(ref, i):
        return ref[i * RANK : (i + 1) * RANK, :]

    up_zero = up_nodes_ref[pl.ds(pl.multiple_of(odd * RANK, RANK), RANK), :]
    chain = None
    outward = []
    for level in range(1, LEVELS):
        to = slice((level - 1) * RANK, level * RANK)
        if chain is None:
            outward.append(node(couple_nodes_ref, level).astype(F32))
            down_path_ref[to, :] = up_zero
            chain = node(up_nodes_ref, 2)
        else:
            outward.append(dot(chain, node(couple_nodes_ref, level)))
            down_path_ref[to, :] = dot(up_zero, chain).astype(BF16)
            if level + 1 < LEVELS:
                chain = dot(chain, node(up_nodes_ref, level + 1)).astype(BF16)
    out_path_ref[...] = jnp.concatenate(outward, axis=1).astype(BF16)
    sb_out.wait()


def pair_kernel(n_sums, own_ref, ra_ref, up_ref, path_ref, out_hbm, block_ref, out_sems):
    position = lax.axis_index("leaf")
    odd = lax.rem(position, 2)
    chip = position >> 1
    own = own_ref[...].astype(F32)
    other = ra_ref[BOX_AT:PAIR_ROWS, :].astype(F32)
    even_side = jnp.where(odd == 0, own, other)
    odd_side = jnp.where(odd == 0, other, own)
    both = own + other
    joined = jnp.concatenate([even_side[:, :RANK], odd_side[:, :RANK]], axis=1).astype(BF16)
    moment = dot(joined, up_ref[...]).astype(BF16)
    levels = dot(moment, path_ref[...])
    sums = sums_block([read_sum(both, j) for j in range(n_sums)])
    low = lanes() < RANK
    outs = []
    at = 0
    for level in range(LEVELS):
        count = 1 if level == 0 else 1 << (level - 1)
        if level == 0:
            block, first = sums, chip
        else:
            group = levels[:, (level - 1) // 2 * 128 : (level + 1) // 2 * 128]
            if level % 2 == 0:
                group = pltpu.roll(group, RANK, 1)
            block = jnp.where(low, group, sums)
            first = ((chip >> (level - 1)) ^ 1) << (level - 1)
        block = block.astype(BF16)
        copies = min(count, COPIES)
        for c in range(copies):
            block_ref[at + c] = block
        for i in range(count // copies):
            out = pltpu.make_async_copy(
                block_ref.at[pl.ds(at, copies)],
                out_hbm.at[pl.ds(first + i * copies, copies)],
                out_sems.at[len(outs)],
            )
            out.start()
            outs.append(out)
        at += copies
    for out in outs:
        out.wait()


def near_far_kernel(
    near_index_hbm,
    far_index_hbm,
    sb_hbm,
    mom_ref,
    ra_any,
    rb_any,
    tile_hbm,
    couple_ref,
    near_hbm,
    far_ref,
    near_index_ref,
    far_index_ref,
    near_ref,
    x_ref,
    ra_ref,
    rb_ref,
    left_ref,
    right_ref,
    tile_ref,
    in_sems,
    tile_sems,
    near_sems,
):
    small = start_copies(
        (rb_any, ra_any, sb_hbm, near_index_hbm, far_index_hbm),
        (
            rb_ref,
            ra_ref,
            x_ref.at[pl.ds(REACH, SLOTS)],
            near_index_ref,
            far_index_ref,
        ),
        in_sems,
    )
    parts = [pl.ds(sum(GROUPS[:i]), size) for i, size in enumerate(GROUPS)]
    tiles = start_copies(
        [tile_hbm.at[part] for part in parts], [tile_ref.at[part] for part in parts], tile_sems
    )
    position = lax.axis_index("leaf")
    odd = lax.rem(position, 2)
    low = lanes() < RANK

    def spread_moments(source, first):
        for j in range(HALF):
            both = source[j * RHS : (j + 1) * RHS, :].astype(F32)
            turned = pltpu.roll(both, RANK, 1)
            left_ref[first + 2 * j] = jnp.where(low, both, 0.0).astype(BF16)
            right_ref[first + 2 * j] = jnp.where(low, 0.0, turned).astype(BF16)
            left_ref[first + 2 * j + 1] = jnp.where(low, turned, 0.0).astype(BF16)
            right_ref[first + 2 * j + 1] = jnp.where(low, 0.0, both).astype(BF16)

    def edges(source, first):
        for j in range(REACH):
            for half in range(2):
                start = MOM_ROWS + (2 * j + half) * RHS
                x_ref[first + j, :, half * 128 : (half + 1) * 128] = source[start : start + RHS, :]

    spread_moments(mom_ref, SLOTS)
    for copy in small:
        copy.wait()
    spread_moments(rb_ref, odd * (2 * SLOTS))
    spread_moments(ra_ref, (1 - odd) * (2 * SLOTS))
    edges(rb_ref, odd * (REACH + SLOTS))
    edges(ra_ref, (1 - odd) * (REACH + SLOTS))
    near_base = position * SLOTS - REACH
    far_base = position * SLOTS - SLOTS
    for g in range(SLOTS):
        pairs = [
            left_ref[far_index_ref[2 * f, g] - far_base]
            + right_ref[far_index_ref[2 * f + 1, g] - far_base]
            for f in range(4)
        ]
        far_ref[:, g * RANK : (g + 1) * RANK] = dot(jnp.concatenate(pairs, axis=1), couple_ref[g])
    outs = []
    for i, part in enumerate(parts):
        tiles[i].wait()
        for g in range(part.start, part.start + part.size):
            columns = [x_ref[near_index_ref[k, g] - near_base] for k in range(6)]
            near_ref[g] = dot(jnp.concatenate(columns, axis=1), tile_ref[g])
        out = pltpu.make_async_copy(near_ref.at[part], near_hbm.at[part], near_sems.at[i])
        out.start()
        outs.append(out)
    for out in outs:
        out.wait()


def tree_sweep(ra_ref, gathered_ref, couple_zero_ref, down_path_ref):
    chip = lax.axis_index("leaf") >> 1
    total = gathered_ref[chip].astype(F32)
    sibling = ra_ref[BOX_AT:PAIR_ROWS, :][:, :RANK]
    downward = dot(sibling, couple_zero_ref[...])
    for level in range(1, LEVELS):
        level_sum = jnp.zeros((RHS, 128), F32)
        for x in range(1 << (level - 1), 1 << level):
            level_sum = level_sum + gathered_ref[chip ^ x].astype(F32)
        total = total + level_sum
        path = down_path_ref[(level - 1) * RANK : level * RANK, :]
        downward = downward + dot_nt(level_sum[:, :RANK].astype(BF16), path)
    return downward.astype(BF16), total


def spread_of(downward, far_ref, basis_ref, transfer_ref):
    block = block_of_lane()
    local_total = far_ref[...] + dot_nt(downward, transfer_ref[...])
    spread = []
    for q in range(SLOTS // 4):
        group = local_total[:, 4 * q * RANK : 4 * (q + 1) * RANK]
        apart = jnp.concatenate(
            [jnp.where(block == j, group, 0.0).astype(BF16) for j in range(4)], axis=0
        )
        four = dot(apart, basis_ref[4 * q * RANK : 4 * (q + 1) * RANK, :])
        spread += [four[j * RHS : (j + 1) * RHS, :] for j in range(4)]
    return spread


def middle_kernel(
    ra_ref,
    gathered_ref,
    couple_zero_ref,
    down_path_ref,
    far_ref,
    *refs,
):
    hbm, refs = refs[:5], refs[5:]
    pa_ref, pb_ref, own_ref, scal_ref, sb_hbm, image_hbm, *refs = refs
    local, refs = refs[:5], refs[5:]
    sb_ref, image_ref, sems, out_sems, image_sems = refs
    copies = start_copies(hbm, local, sems)
    live_ref, transfer_ref, basis_ref, near_ref, rh_ref = local
    downward, total = tree_sweep(ra_ref, gathered_ref, couple_zero_ref, down_path_ref)
    for copy in copies:
        copy.wait()
    spread = spread_of(downward, far_ref, basis_ref, transfer_ref)
    outs = []
    square = read_sum(total, 0)
    norm = jnp.sqrt(square + EPSILON)
    scal_ref[...] = jnp.where(lanes() == 0, norm, square)
    inputs = []
    inner = jnp.zeros((RHS, POINTS), F32)
    length = jnp.zeros((RHS, POINTS), F32)
    for g in range(SLOTS):
        image = live_ref[g].astype(F32) * (near_ref[g] + spread[g]) / norm
        image_ref[g] = image
        if g % 4 == 3:
            four = pl.ds(g - 3, 4)
            out = pltpu.make_async_copy(
                image_ref.at[four], image_hbm.at[four], image_sems.at[g // 4]
            )
            out.start()
            outs.append(out)
        basis_one = rh_ref[g] * live_ref[g].astype(F32) / norm
        inner = inner + basis_one * image
        length = length + image * image
        sb = image.astype(BF16)
        sb_ref[g] = sb
        inputs.append(sb)
    outs += start_copies((sb_ref,), (sb_hbm,), out_sems)
    moments, box = up_moments(inputs, basis_ref, transfer_ref)
    pack_out(inputs, moments, box, [row_sum(inner), row_sum(length)], pa_ref, pb_ref, own_ref)
    for out in outs:
        out.wait()


def as_row(column, shift):
    return jnp.sum(jnp.where(lanes() == rows() + shift, column, 0.0), axis=0, keepdims=True)


def as_column(row, shift):
    return row_sum(jnp.where(lanes() == rows() + shift, row, 0.0))


def last_operator_kernel(
    ra_ref,
    gathered_ref,
    couple_zero_ref,
    down_path_ref,
    scal_in_ref,
    far_ref,
    *refs,
):
    hbm, refs = refs[:6], refs[6:]
    one_ref, two_ref, v_ref, send_ref, scal_ref, *refs = refs
    local, (sems,) = refs[:6], refs[6:]
    copies = start_copies(hbm, local, sems)
    live_ref, transfer_ref, basis_ref, near_ref, rh_ref, image_ref = local
    downward, total = tree_sweep(ra_ref, gathered_ref, couple_zero_ref, down_path_ref)
    for copy in copies:
        copy.wait()
    spread = spread_of(downward, far_ref, basis_ref, transfer_ref)
    norm = scal_in_ref[:, 0:1]
    one_one = (scal_in_ref[:, 1:2] / norm) / norm
    first_inner = read_sum(total, 0)
    image_square = read_sum(total, 1)
    residue = image_square - 2.0 * first_inner * first_inner + first_inner * first_inner * one_one
    residue = jnp.maximum(residue, 0.0)
    first_length = jnp.sqrt(residue + EPSILON)
    one_two = (first_inner - first_inner * one_one) / first_length
    two_two = (residue / first_length) / first_length
    at = lanes()
    scal = jnp.zeros((RHS, 128), F32)
    for j, column in enumerate((norm, first_inner, first_length, one_one, one_two, two_two)):
        scal = jnp.where(at == j, column, scal)
    scal_ref[...] = scal
    cross = jnp.zeros((RHS, POINTS), F32)
    own = jnp.zeros((RHS, POINTS), F32)
    square = jnp.zeros((RHS, POINTS), F32)
    for g in range(SLOTS):
        image = image_ref[g]
        y = live_ref[g].astype(F32) * (near_ref[g] + spread[g])
        basis_one = rh_ref[g] * live_ref[g].astype(F32) / norm
        basis_two = (image - first_inner * basis_one) / first_length
        v = (y - first_inner * image) / first_length
        one_ref[g] = basis_one
        two_ref[g] = basis_two
        v_ref[g] = v
        cross = cross + basis_one * v
        own = own + basis_two * v
        square = square + v * v
    row = as_row(row_sum(cross), 0) + as_row(row_sum(own), 32) + as_row(row_sum(square), 64)
    for d in range(DEVICES):
        send_ref[d] = row


def final_kernel(one_ref, two_ref, v_ref, scal_ref, gathered_ref, next_ref, hess_ref):
    row = jnp.sum(gathered_ref[...], axis=0)
    cross, own, square = as_column(row, 0), as_column(row, 32), as_column(row, 64)
    norm, first_inner, first_length, one_one, one_two, two_two = (
        scal_ref[:, j : j + 1] for j in range(6)
    )
    residue = (
        square
        - 2.0 * cross * cross
        - 2.0 * own * own
        + cross * cross * one_one
        + own * own * two_two
        + 2.0 * cross * own * one_two
    )
    second_length = jnp.sqrt(jnp.maximum(residue, 0.0) + EPSILON)
    for j, column in enumerate((norm, first_inner, first_length, cross, own, second_length)):
        hess_ref[j : j + 1, :] = as_row(column, 0)[:, :RHS]
    for g in range(SLOTS):
        next_ref[g] = (v_ref[g] - cross * one_ref[g] - own * two_ref[g]) / second_length


def shape(dims, dtype):
    return jax.ShapeDtypeStruct(dims, dtype)


FIELD = (SLOTS, RHS, POINTS)
FAR_FIELD = (RHS, SLOTS * RANK)
PACKED = [shape((PAIR_ROWS, 128), BF16), shape((BOX_AT, 128), BF16), shape((RHS, 128), BF16)]
BASIS = (SLOTS * RANK, POINTS)
TRANSFER = (SLOTS * RANK, RANK)
TURNED = (RANK * RANK, NODES)
GATHERED = (CHIPS, RHS, 128)
LEAF_BUFFERS = [(TRANSFER, BF16), (BASIS, BF16), (FIELD, F32), (FIELD, F32)]
PATH = (LEVELS - 1) * RANK
WEIGHTS = [
    shape((2 * RANK, RANK), BF16),
    shape((RANK, RANK), BF16),
    shape((RANK, PATH), BF16),
    shape((PATH, RANK), BF16),
]
MIB = 1 << 20


def vmem(*kinds):
    return [pltpu.VMEM(*kind) for kind in kinds]


def sems(*dims):
    return [pltpu.SemaphoreType.DMA(dim) for dim in dims]


def in_hbm(*arrays):
    return [pltpu.with_memory_space_constraint(array, pltpu.HBM) for array in arrays]


def call(kernel, outs, in_specs, out_specs, scratch, mib, **more):
    return pl.pallas_call(
        kernel,
        out_shape=outs,
        in_specs=in_specs,
        out_specs=out_specs,
        scratch_shapes=scratch,
        compiler_params=pltpu.CompilerParams(vmem_limit_bytes=mib * MIB),
        **more,
    )


def on_device(
    right_hand,
    leaf_live,
    near_index,
    near_tile,
    far_index,
    far_couple,
    leaf_basis,
    leaf_transfer,
    tree_up,
    tree_couple,
):
    up_turned = tree_up.transpose(1, 2, 0).reshape(TURNED)
    couple_turned = tree_couple.transpose(1, 2, 0).reshape(TURNED)
    tiles = near_tile.reshape(SLOTS, 6 * POINTS, POINTS)
    couples = far_couple.reshape(SLOTS, 8 * RANK, RANK)
    indices = (near_index.T, far_index.T)
    leaf_basis = leaf_basis.reshape(BASIS)
    leaf_transfer = leaf_transfer.reshape(TRANSFER)
    same = [(i, i ^ 1) for i in range(DEVICES)]
    across = [(i, (i + 1) % DEVICES) for i in range(1, DEVICES, 2)]
    across += [(j, i) for i, j in across]
    groups = [[2 * c + core for c in range(CHIPS)] for core in range(2)]

    def exchange(pa, pb, own, pair_up, out_path, n_sums):
        ra = lax.ppermute(pa, "leaf", same)
        rb = lax.ppermute(pb, "leaf", across)
        sent = call(
            functools.partial(pair_kernel, n_sums),
            pltpu.HBM(GATHERED, BF16),
            [VMEM] * 4,
            HBM,
            [*vmem(((4 * COPIES, RHS, 128), BF16)), *sems((11,))],
            4,
        )(own, ra, pair_up, out_path)
        gathered = lax.all_to_all(sent, "leaf", 0, 0, axis_index_groups=groups)
        return ra, rb, gathered

    def near_far(sb, pb, ra, rb):
        return call(
            near_far_kernel,
            [pltpu.HBM(FIELD, F32), shape(FAR_FIELD, F32)],
            [HBM, HBM, HBM, VMEM, ANY, ANY, HBM, VMEM],
            [HBM, VMEM],
            [
                pltpu.SMEM((6, SLOTS), jnp.int32),
                pltpu.SMEM((8, SLOTS), jnp.int32),
                *vmem(
                    (FIELD, F32),
                    ((SLOTS + 2 * REACH, RHS, POINTS), BF16),
                    ((PAIR_ROWS, 128), BF16),
                    ((BOX_AT, 128), BF16),
                    ((3 * SLOTS, RHS, 128), BF16),
                    ((3 * SLOTS, RHS, 128), BF16),
                    ((SLOTS, 6 * POINTS, POINTS), BF16),
                ),
                *sems((5,), (len(GROUPS),), (len(GROUPS),)),
            ],
            40,
            cost_estimate=pl.CostEstimate(
                flops=1_000_000_000, bytes_accessed=16_000_000, transcendentals=0
            ),
        )(*in_hbm(*indices, sb), pb, ra, rb, *in_hbm(tiles), couples)

    pa, pb, own, sb, pair_up, couple_zero, out_path, down_path = call(
        first_kernel,
        [*PACKED, pltpu.HBM(FIELD, BF16), *WEIGHTS],
        [HBM] * 6,
        [VMEM] * 3 + [HBM] + [VMEM] * 4,
        [
            pltpu.SMEM((SLOTS,), jnp.int32),
            *vmem(
                (FIELD, F32),
                (BASIS, BF16),
                (TRANSFER, BF16),
                (TURNED, BF16),
                (TURNED, BF16),
                (FIELD, BF16),
                ((8 * RANK, RANK), BF16),
                ((8 * RANK, RANK), BF16),
                ((8 * RANK, RANK), F32),
                ((8 * RANK, RANK), F32),
            ),
            *sems((6,)),
            pltpu.SemaphoreType.DMA,
        ],
        16,
    )(*in_hbm(leaf_live, right_hand, leaf_basis, leaf_transfer, up_turned, couple_turned))
    ra, rb, gathered = exchange(pa, pb, own, pair_up, out_path, 1)
    near, far = near_far(sb, pb, ra, rb)
    count = len(LEAF_BUFFERS)
    pa, pb, own, scal, sb, image = call(
        middle_kernel,
        [
            *PACKED,
            shape((RHS, 128), F32),
            pltpu.HBM(FIELD, BF16),
            pltpu.HBM(FIELD, F32),
        ],
        [VMEM] * 5 + [HBM] * (count + 1),
        [VMEM] * 4 + [HBM] * 2,
        [
            pltpu.SMEM((SLOTS,), jnp.int32),
            *vmem(*LEAF_BUFFERS, (FIELD, BF16), (FIELD, F32)),
            *sems((count + 1,), (1,), (4,)),
        ],
        16,
    )(
        ra, gathered, couple_zero, down_path, far,
        *in_hbm(leaf_live, leaf_transfer, leaf_basis, near, right_hand),
    )
    ra, rb, gathered = exchange(pa, pb, own, pair_up, out_path, 2)
    near, far = near_far(sb, pb, ra, rb)
    one, two, v, sent, scal = call(
        last_operator_kernel,
        [shape(FIELD, F32)] * 3 + [shape((DEVICES, 1, 128), F32), shape((RHS, 128), F32)],
        [VMEM] * 6 + [HBM] * (count + 2),
        [VMEM] * 5,
        [
            pltpu.SMEM((SLOTS,), jnp.int32),
            *vmem(*LEAF_BUFFERS, (FIELD, F32)),
            *sems((count + 2,)),
        ],
        16,
    )(
        ra, gathered, couple_zero, down_path, scal, far,
        *in_hbm(leaf_live, leaf_transfer, leaf_basis, near, right_hand, image),
    )
    gathered = lax.all_to_all(sent, "leaf", 0, 0)
    return call(
        final_kernel, [shape(FIELD, F32), shape((6, RHS), F32)], [VMEM] * 5, [VMEM] * 2, [], 8
    )(one, two, v, scal, gathered)


def solution(mesh):
    placed = (
        P("leaf", None, None),
        P("leaf"),
        P("leaf", None),
        P("leaf", None, None, None),
        P("leaf", None),
        P("leaf", None, None, None),
        P("leaf", None, None),
        P("leaf", None, None),
        P(),
        P(),
    )
    return jax.shard_map(
        on_device,
        mesh=mesh,
        in_specs=placed,
        out_specs=(P("leaf", None, None), P()),
        check_vma=False,
    )
```

```python
import functools

import jax
import jax.numpy as jnp
from jax import lax
from jax.experimental import pallas as pl
from jax.experimental.pallas import tpu as pltpu
from jax.sharding import PartitionSpec as P


EPSILON = 1e-06
F32 = jnp.float32
BF16 = jnp.bfloat16
NT = (((1,), (1,)), ((), ()))

ANY = pl.BlockSpec(memory_space=pl.ANY)
VMEM = pl.BlockSpec(memory_space=pltpu.VMEM)
HBM = pl.BlockSpec(memory_space=pltpu.HBM)

SLOTS, RHS, POINTS, RANK = 16, 32, 256, 64
REACH = 2
HALF = SLOTS // 2
MOM_ROWS = HALF * RHS
NEAR_ROWS = REACH * 2 * RHS
BOX_AT = MOM_ROWS + NEAR_ROWS
PAIR_ROWS = BOX_AT + RHS
DEVICES = 128
LEVELS = 7
CHIPS = DEVICES // 2
NODES = 254
GROUPS = (4, 4, 4, 2, 2)
COPIES = 8


def dot(a, b):
    return jnp.dot(a, b, preferred_element_type=F32)


def dot_nt(a, b):
    return lax.dot_general(a, b, NT, preferred_element_type=F32)


def row_sum(x):
    return jnp.sum(x, axis=1, keepdims=True)


def lanes(shape=(RHS, 128)):
    return lax.broadcasted_iota(jnp.int32, shape, 1)


def rows(shape=(RHS, 128)):
    return lax.broadcasted_iota(jnp.int32, shape, 0)


def level_start(level):
    return 2 * DEVICES - 2 * (DEVICES >> level)


def three_parts(column):
    high = column.astype(BF16).astype(F32)
    rest = column - high
    middle = rest.astype(BF16).astype(F32)
    low = (rest - middle).astype(BF16).astype(F32)
    return high, middle, low


def sums_block(sums):
    at = lanes()
    block = jnp.zeros((RHS, 128), F32)
    for j, column in enumerate(sums):
        for k, part in enumerate(three_parts(column)):
            block = jnp.where(at == RANK + 3 * j + k, part, block)
    return block


def message(moment, sums):
    wide = jnp.concatenate([moment, jnp.zeros((RHS, 128 - RANK), F32)], axis=1)
    return jnp.where(lanes() < RANK, wide, sums_block(sums)).astype(BF16)


def read_sum(block, j):
    at = lanes()
    first = RANK + 3 * j
    return row_sum(jnp.where((at >= first) & (at < first + 3), block, 0.0))


def pack_out(inputs, moments, box, sums, pa_ref, pb_ref, own_ref):
    block = message(box, sums)
    own_ref[...] = block
    pa_ref[BOX_AT:PAIR_ROWS, :] = block
    for j in range(HALF):
        both = moments[:, j * 128 : (j + 1) * 128]
        pa_ref[j * RHS : (j + 1) * RHS, :] = both
        pb_ref[j * RHS : (j + 1) * RHS, :] = both
    odd = lax.rem(lax.axis_index("leaf"), 2)

    def edge(ref, first):
        for j in range(REACH):
            x = inputs[first + j]
            for half in range(2):
                start = MOM_ROWS + (2 * j + half) * RHS
                ref[start : start + RHS, :] = x[:, half * 128 : (half + 1) * 128]

    @pl.when(odd == 0)
    def _():
        edge(pa_ref, SLOTS - REACH)
        edge(pb_ref, 0)

    @pl.when(odd == 1)
    def _():
        edge(pa_ref, 0)
        edge(pb_ref, SLOTS - REACH)


def block_of_lane():
    return lanes((RHS, 4 * RANK)) // RANK


def up_moments(inputs, basis_ref, transfer_ref):
    block = block_of_lane()
    groups = []
    for q in range(SLOTS // 4):
        four = jnp.concatenate(inputs[4 * q : 4 * q + 4], axis=0)
        crossed = dot_nt(four, basis_ref[4 * q * RANK : 4 * (q + 1) * RANK, :])
        group = crossed[0:RHS, :]
        for j in range(1, 4):
            group = jnp.where(block == j, crossed[j * RHS : (j + 1) * RHS, :], group)
        groups.append(group.astype(BF16))
    moments = jnp.concatenate(groups, axis=1)
    return moments, dot(moments, transfer_ref[...])


def start_copies(sources, targets, sems):
    copies = [
        pltpu.make_async_copy(source, target, sems.at[i])
        for i, (source, target) in enumerate(zip(sources, targets, strict=True))
    ]
    for copy in copies:
        copy.start()
    return copies


def one_hot(count, nodes):
    at, row = lanes((count, NODES)), rows((count, NODES))
    block = jnp.zeros((count, NODES), F32)
    for i, node in enumerate(nodes):
        block = jnp.where((row == i) & (at == node), 1.0, block)
    return block.astype(BF16)


def pick_nodes(nodes, turned_ref, out_ref, rows_ref):
    pick = one_hot(8, nodes)
    for k in range(0, RANK, 4):
        four = dot_nt(pick, turned_ref[k * RANK : (k + 4) * RANK, :])
        for j in range(4):
            rows_ref[pl.ds(k + j, 8, stride=RANK), :] = four[:, j * RANK : (j + 1) * RANK]
    out_ref[...] = rows_ref[...].astype(BF16)


def first_kernel(
    live_hbm,
    rh_hbm,
    basis_hbm,
    transfer_hbm,
    up_hbm,
    couple_hbm,
    pa_ref,
    pb_ref,
    own_ref,
    sb_hbm,
    pair_ref,
    couple_zero_ref,
    out_path_ref,
    down_path_ref,
    live_ref,
    rh_ref,
    basis_ref,
    transfer_ref,
    up_ref,
    couple_ref,
    sb_ref,
    up_nodes_ref,
    couple_nodes_ref,
    up_rows_ref,
    couple_rows_ref,
    sems,
    out_sem,
):
    up_in, couple_in, *copies = start_copies(
        (up_hbm, couple_hbm, live_hbm, rh_hbm, basis_hbm, transfer_hbm),
        (up_ref, couple_ref, live_ref, rh_ref, basis_ref, transfer_ref),
        sems,
    )
    position = lax.axis_index("leaf")
    odd = lax.rem(position, 2)
    path = [level_start(level) + (position >> level) for level in range(1, LEVELS - 1)]
    beside = [level_start(level) + ((position >> level) ^ 1) for level in range(1, LEVELS)]
    up_in.wait()
    pick_nodes((position - odd, position - odd + 1, *path), up_ref, up_nodes_ref, up_rows_ref)
    couple_in.wait()
    pick_nodes((position, *beside), couple_ref, couple_nodes_ref, couple_rows_ref)
    for copy in copies:
        copy.wait()
    inputs = []
    square = jnp.zeros((RHS, POINTS), F32)
    for g in range(SLOTS):
        s = rh_ref[g] * live_ref[g].astype(F32)
        square = square + s * s
        sb = s.astype(BF16)
        sb_ref[g] = sb
        inputs.append(sb)
    sb_out = pltpu.make_async_copy(sb_ref, sb_hbm, out_sem)
    sb_out.start()
    moments, box = up_moments(inputs, basis_ref, transfer_ref)
    pack_out(inputs, moments, box, [row_sum(square)], pa_ref, pb_ref, own_ref)
    pair_ref[...] = up_nodes_ref[0 : 2 * RANK, :]
    couple_zero_ref[...] = couple_nodes_ref[0:RANK, :]

    def node(ref, i):
        return ref[i * RANK : (i + 1) * RANK, :]

    up_zero = up_nodes_ref[pl.ds(pl.multiple_of(odd * RANK, RANK), RANK), :]
    chain = None
    outward = []
    for level in range(1, LEVELS):
        to = slice((level - 1) * RANK, level * RANK)
        if chain is None:
            outward.append(node(couple_nodes_ref, level).astype(F32))
            down_path_ref[to, :] = up_zero
            chain = node(up_nodes_ref, 2)
        else:
            outward.append(dot(chain, node(couple_nodes_ref, level)))
            down_path_ref[to, :] = dot(up_zero, chain).astype(BF16)
            if level + 1 < LEVELS:
                chain = dot(chain, node(up_nodes_ref, level + 1)).astype(BF16)
    out_path_ref[...] = jnp.concatenate(outward, axis=1).astype(BF16)
    sb_out.wait()


def pair_kernel(n_sums, own_ref, ra_ref, up_ref, path_ref, out_hbm, block_ref, out_sems):
    position = lax.axis_index("leaf")
    odd = lax.rem(position, 2)
    chip = position >> 1
    own = own_ref[...].astype(F32)
    other = ra_ref[BOX_AT:PAIR_ROWS, :].astype(F32)
    even_side = jnp.where(odd == 0, own, other)
    odd_side = jnp.where(odd == 0, other, own)
    both = own + other
    joined = jnp.concatenate([even_side[:, :RANK], odd_side[:, :RANK]], axis=1).astype(BF16)
    moment = dot(joined, up_ref[...]).astype(BF16)
    levels = dot(moment, path_ref[...])
    parts = [part for j in range(n_sums) for part in three_parts(read_sum(both, j))]
    sums = jnp.zeros((8, 128), F32)
    for p, part in enumerate(parts):
        sums = jnp.where(rows((8, 128)) == p, as_row(part, 0), sums)
    half = RHS // 2
    low = lanes((half, 128)) < RANK
    outs = []
    at = 0
    for level in range(LEVELS):
        count = 1 if level == 0 else 1 << (level - 1)
        if level == 0:
            packed, first = jnp.zeros((half, 128), F32), chip
        else:
            group = levels[:, (level - 1) // 2 * 128 : (level + 1) // 2 * 128]
            turned = pltpu.roll(group, RANK, 1)
            if level % 2 == 0:
                group, turned = turned, group
            packed = jnp.where(low, group[:half], turned[half:])
            first = ((chip >> (level - 1)) ^ 1) << (level - 1)
        block = jnp.concatenate([packed, sums], axis=0).astype(BF16)
        copies = min(count, COPIES)
        for c in range(copies):
            block_ref[at + c] = block
        for i in range(count // copies):
            out = pltpu.make_async_copy(
                block_ref.at[pl.ds(at, copies)],
                out_hbm.at[pl.ds(first + i * copies, copies)],
                out_sems.at[len(outs)],
            )
            out.start()
            outs.append(out)
        at += copies
    for out in outs:
        out.wait()


def near_far_kernel(
    near_index_hbm,
    far_index_hbm,
    sb_hbm,
    mom_ref,
    ra_any,
    rb_any,
    tile_hbm,
    couple_ref,
    near_hbm,
    far_ref,
    near_index_ref,
    far_index_ref,
    near_ref,
    x_ref,
    ra_ref,
    rb_ref,
    left_ref,
    right_ref,
    tile_ref,
    in_sems,
    tile_sems,
    near_sems,
):
    small = start_copies(
        (rb_any, ra_any, sb_hbm, near_index_hbm, far_index_hbm),
        (
            rb_ref,
            ra_ref,
            x_ref.at[pl.ds(REACH, SLOTS)],
            near_index_ref,
            far_index_ref,
        ),
        in_sems,
    )
    parts = [pl.ds(sum(GROUPS[:i]), size) for i, size in enumerate(GROUPS)]
    tiles = start_copies(
        [tile_hbm.at[part] for part in parts], [tile_ref.at[part] for part in parts], tile_sems
    )
    position = lax.axis_index("leaf")
    odd = lax.rem(position, 2)
    low = lanes() < RANK

    def spread_moments(source, first):
        for j in range(HALF):
            both = source[j * RHS : (j + 1) * RHS, :].astype(F32)
            turned = pltpu.roll(both, RANK, 1)
            left_ref[first + 2 * j] = jnp.where(low, both, 0.0).astype(BF16)
            right_ref[first + 2 * j] = jnp.where(low, 0.0, turned).astype(BF16)
            left_ref[first + 2 * j + 1] = jnp.where(low, turned, 0.0).astype(BF16)
            right_ref[first + 2 * j + 1] = jnp.where(low, 0.0, both).astype(BF16)

    def edges(source, first):
        for j in range(REACH):
            for half in range(2):
                start = MOM_ROWS + (2 * j + half) * RHS
                x_ref[first + j, :, half * 128 : (half + 1) * 128] = source[start : start + RHS, :]

    spread_moments(mom_ref, SLOTS)
    for copy in small:
        copy.wait()
    spread_moments(rb_ref, odd * (2 * SLOTS))
    spread_moments(ra_ref, (1 - odd) * (2 * SLOTS))
    edges(rb_ref, odd * (REACH + SLOTS))
    edges(ra_ref, (1 - odd) * (REACH + SLOTS))
    near_base = position * SLOTS - REACH
    far_base = position * SLOTS - SLOTS
    for g in range(SLOTS):
        pairs = [
            left_ref[far_index_ref[2 * f, g] - far_base]
            + right_ref[far_index_ref[2 * f + 1, g] - far_base]
            for f in range(4)
        ]
        far_ref[:, g * RANK : (g + 1) * RANK] = dot(jnp.concatenate(pairs, axis=1), couple_ref[g])
    outs = []
    for i, part in enumerate(parts):
        tiles[i].wait()
        for g in range(part.start, part.start + part.size):
            columns = [x_ref[near_index_ref[k, g] - near_base] for k in range(6)]
            near_ref[g] = dot(jnp.concatenate(columns, axis=1), tile_ref[g])
        out = pltpu.make_async_copy(near_ref.at[part], near_hbm.at[part], near_sems.at[i])
        out.start()
        outs.append(out)
    for out in outs:
        out.wait()


def tree_sweep(ra_ref, gathered_ref, couple_zero_ref, down_path_ref):
    chip = lax.axis_index("leaf") >> 1
    total = gathered_ref[chip].astype(F32)
    sibling = ra_ref[BOX_AT:PAIR_ROWS, :][:, :RANK]
    downward = dot(sibling, couple_zero_ref[...])
    for level in range(1, LEVELS):
        level_sum = jnp.zeros(GATHERED[1:], F32)
        for x in range(1 << (level - 1), 1 << level):
            level_sum = level_sum + gathered_ref[chip ^ x].astype(F32)
        total = total + level_sum
        path = down_path_ref[(level - 1) * RANK : level * RANK, :]
        packed = level_sum[: RHS // 2]
        local = jnp.concatenate([packed[:, :RANK], packed[:, RANK:]], axis=0)
        downward = downward + dot_nt(local.astype(BF16), path)
    return downward.astype(BF16), total


def gathered_sum(total, j):
    row = rows((8, 128))
    parts = jnp.where((row >= 3 * j) & (row < 3 * j + 3), total[RHS // 2 :], 0.0)
    return as_column(jnp.sum(parts, axis=0, keepdims=True), 0)


def spread_of(downward, far_ref, basis_ref, transfer_ref):
    block = block_of_lane()
    local_total = far_ref[...] + dot_nt(downward, transfer_ref[...])
    spread = []
    for q in range(SLOTS // 4):
        group = local_total[:, 4 * q * RANK : 4 * (q + 1) * RANK]
        apart = jnp.concatenate(
            [jnp.where(block == j, group, 0.0).astype(BF16) for j in range(4)], axis=0
        )
        four = dot(apart, basis_ref[4 * q * RANK : 4 * (q + 1) * RANK, :])
        spread += [four[j * RHS : (j + 1) * RHS, :] for j in range(4)]
    return spread


def middle_kernel(
    ra_ref,
    gathered_ref,
    couple_zero_ref,
    down_path_ref,
    far_ref,
    *refs,
):
    hbm, refs = refs[:5], refs[5:]
    pa_ref, pb_ref, own_ref, scal_ref, sb_hbm, image_hbm, *refs = refs
    local, refs = refs[:5], refs[5:]
    sb_ref, image_ref, sems, out_sems, image_sems = refs
    copies = start_copies(hbm, local, sems)
    live_ref, transfer_ref, basis_ref, near_ref, rh_ref = local
    downward, total = tree_sweep(ra_ref, gathered_ref, couple_zero_ref, down_path_ref)
    for copy in copies:
        copy.wait()
    spread = spread_of(downward, far_ref, basis_ref, transfer_ref)
    outs = []
    square = gathered_sum(total, 0)
    norm = jnp.sqrt(square + EPSILON)
    scal_ref[...] = jnp.where(lanes() == 0, norm, square)
    inputs = []
    inner = jnp.zeros((RHS, POINTS), F32)
    length = jnp.zeros((RHS, POINTS), F32)
    for g in range(SLOTS):
        image = live_ref[g].astype(F32) * (near_ref[g] + spread[g]) / norm
        image_ref[g] = image
        if g % 4 == 3:
            four = pl.ds(g - 3, 4)
            out = pltpu.make_async_copy(
                image_ref.at[four], image_hbm.at[four], image_sems.at[g // 4]
            )
            out.start()
            outs.append(out)
        basis_one = rh_ref[g] * live_ref[g].astype(F32) / norm
        inner = inner + basis_one * image
        length = length + image * image
        sb = image.astype(BF16)
        sb_ref[g] = sb
        inputs.append(sb)
    outs += start_copies((sb_ref,), (sb_hbm,), out_sems)
    moments, box = up_moments(inputs, basis_ref, transfer_ref)
    pack_out(inputs, moments, box, [row_sum(inner), row_sum(length)], pa_ref, pb_ref, own_ref)
    for out in outs:
        out.wait()


def as_row(column, shift):
    return jnp.sum(jnp.where(lanes() == rows() + shift, column, 0.0), axis=0, keepdims=True)


def as_column(row, shift):
    return row_sum(jnp.where(lanes() == rows() + shift, row, 0.0))


def last_operator_kernel(
    ra_ref,
    gathered_ref,
    couple_zero_ref,
    down_path_ref,
    scal_in_ref,
    far_ref,
    *refs,
):
    hbm, refs = refs[:6], refs[6:]
    one_ref, two_ref, v_ref, send_ref, scal_ref, *refs = refs
    local, (sems,) = refs[:6], refs[6:]
    copies = start_copies(hbm, local, sems)
    live_ref, transfer_ref, basis_ref, near_ref, rh_ref, image_ref = local
    downward, total = tree_sweep(ra_ref, gathered_ref, couple_zero_ref, down_path_ref)
    for copy in copies:
        copy.wait()
    spread = spread_of(downward, far_ref, basis_ref, transfer_ref)
    norm = scal_in_ref[:, 0:1]
    one_one = (scal_in_ref[:, 1:2] / norm) / norm
    first_inner = gathered_sum(total, 0)
    image_square = gathered_sum(total, 1)
    residue = image_square - 2.0 * first_inner * first_inner + first_inner * first_inner * one_one
    residue = jnp.maximum(residue, 0.0)
    first_length = jnp.sqrt(residue + EPSILON)
    one_two = (first_inner - first_inner * one_one) / first_length
    two_two = (residue / first_length) / first_length
    at = lanes()
    scal = jnp.zeros((RHS, 128), F32)
    for j, column in enumerate((norm, first_inner, first_length, one_one, one_two, two_two)):
        scal = jnp.where(at == j, column, scal)
    scal_ref[...] = scal
    cross = jnp.zeros((RHS, POINTS), F32)
    own = jnp.zeros((RHS, POINTS), F32)
    square = jnp.zeros((RHS, POINTS), F32)
    for g in range(SLOTS):
        image = image_ref[g]
        y = live_ref[g].astype(F32) * (near_ref[g] + spread[g])
        basis_one = rh_ref[g] * live_ref[g].astype(F32) / norm
        basis_two = (image - first_inner * basis_one) / first_length
        v = (y - first_inner * image) / first_length
        one_ref[g] = basis_one
        two_ref[g] = basis_two
        v_ref[g] = v
        cross = cross + basis_one * v
        own = own + basis_two * v
        square = square + v * v
    row = as_row(row_sum(cross), 0) + as_row(row_sum(own), 32) + as_row(row_sum(square), 64)
    for d in range(DEVICES):
        send_ref[d] = row


def final_kernel(one_ref, two_ref, v_ref, scal_ref, gathered_ref, next_ref, hess_ref):
    row = jnp.sum(gathered_ref[...], axis=0)
    cross, own, square = as_column(row, 0), as_column(row, 32), as_column(row, 64)
    norm, first_inner, first_length, one_one, one_two, two_two = (
        scal_ref[:, j : j + 1] for j in range(6)
    )
    residue = (
        square
        - 2.0 * cross * cross
        - 2.0 * own * own
        + cross * cross * one_one
        + own * own * two_two
        + 2.0 * cross * own * one_two
    )
    second_length = jnp.sqrt(jnp.maximum(residue, 0.0) + EPSILON)
    for j, column in enumerate((norm, first_inner, first_length, cross, own, second_length)):
        hess_ref[j : j + 1, :] = as_row(column, 0)[:, :RHS]
    for g in range(SLOTS):
        next_ref[g] = (v_ref[g] - cross * one_ref[g] - own * two_ref[g]) / second_length


def shape(dims, dtype):
    return jax.ShapeDtypeStruct(dims, dtype)


FIELD = (SLOTS, RHS, POINTS)
FAR_FIELD = (RHS, SLOTS * RANK)
PACKED = [shape((PAIR_ROWS, 128), BF16), shape((BOX_AT, 128), BF16), shape((RHS, 128), BF16)]
BASIS = (SLOTS * RANK, POINTS)
TRANSFER = (SLOTS * RANK, RANK)
TURNED = (RANK * RANK, NODES)
GATHERED = (CHIPS, RHS // 2 + 8, 128)
LEAF_BUFFERS = [(TRANSFER, BF16), (BASIS, BF16), (FIELD, F32), (FIELD, F32)]
PATH = (LEVELS - 1) * RANK
WEIGHTS = [
    shape((2 * RANK, RANK), BF16),
    shape((RANK, RANK), BF16),
    shape((RANK, PATH), BF16),
    shape((PATH, RANK), BF16),
]
MIB = 1 << 20


def vmem(*kinds):
    return [pltpu.VMEM(*kind) for kind in kinds]


def sems(*dims):
    return [pltpu.SemaphoreType.DMA(dim) for dim in dims]


def in_hbm(*arrays):
    return [pltpu.with_memory_space_constraint(array, pltpu.HBM) for array in arrays]


def call(kernel, outs, in_specs, out_specs, scratch, mib, **more):
    return pl.pallas_call(
        kernel,
        out_shape=outs,
        in_specs=in_specs,
        out_specs=out_specs,
        scratch_shapes=scratch,
        compiler_params=pltpu.CompilerParams(vmem_limit_bytes=mib * MIB),
        **more,
    )


def on_device(
    right_hand,
    leaf_live,
    near_index,
    near_tile,
    far_index,
    far_couple,
    leaf_basis,
    leaf_transfer,
    tree_up,
    tree_couple,
):
    up_turned = tree_up.transpose(1, 2, 0).reshape(TURNED)
    couple_turned = tree_couple.transpose(1, 2, 0).reshape(TURNED)
    tiles = near_tile.reshape(SLOTS, 6 * POINTS, POINTS)
    couples = far_couple.reshape(SLOTS, 8 * RANK, RANK)
    indices = (near_index.T, far_index.T)
    leaf_basis = leaf_basis.reshape(BASIS)
    leaf_transfer = leaf_transfer.reshape(TRANSFER)
    same = [(i, i ^ 1) for i in range(DEVICES)]
    across = [(i, (i + 1) % DEVICES) for i in range(1, DEVICES, 2)]
    across += [(j, i) for i, j in across]
    groups = [[2 * c + core for c in range(CHIPS)] for core in range(2)]

    def exchange(pa, pb, own, pair_up, out_path, n_sums):
        ra = lax.ppermute(pa, "leaf", same)
        rb = lax.ppermute(pb, "leaf", across)
        sent = call(
            functools.partial(pair_kernel, n_sums),
            pltpu.HBM(GATHERED, BF16),
            [VMEM] * 4,
            HBM,
            [*vmem(((4 * COPIES, *GATHERED[1:]), BF16)), *sems((11,))],
            4,
        )(own, ra, pair_up, out_path)
        gathered = lax.all_to_all(sent, "leaf", 0, 0, axis_index_groups=groups)
        return ra, rb, gathered

    def near_far(sb, pb, ra, rb):
        return call(
            near_far_kernel,
            [pltpu.HBM(FIELD, F32), shape(FAR_FIELD, F32)],
            [HBM, HBM, HBM, VMEM, ANY, ANY, HBM, VMEM],
            [HBM, VMEM],
            [
                pltpu.SMEM((6, SLOTS), jnp.int32),
                pltpu.SMEM((8, SLOTS), jnp.int32),
                *vmem(
                    (FIELD, F32),
                    ((SLOTS + 2 * REACH, RHS, POINTS), BF16),
                    ((PAIR_ROWS, 128), BF16),
                    ((BOX_AT, 128), BF16),
                    ((3 * SLOTS, RHS, 128), BF16),
                    ((3 * SLOTS, RHS, 128), BF16),
                    ((SLOTS, 6 * POINTS, POINTS), BF16),
                ),
                *sems((5,), (len(GROUPS),), (len(GROUPS),)),
            ],
            40,
            cost_estimate=pl.CostEstimate(
                flops=1_000_000_000, bytes_accessed=16_000_000, transcendentals=0
            ),
        )(*in_hbm(*indices, sb), pb, ra, rb, *in_hbm(tiles), couples)

    pa, pb, own, sb, pair_up, couple_zero, out_path, down_path = call(
        first_kernel,
        [*PACKED, pltpu.HBM(FIELD, BF16), *WEIGHTS],
        [HBM] * 6,
        [VMEM] * 3 + [HBM] + [VMEM] * 4,
        [
            pltpu.SMEM((SLOTS,), jnp.int32),
            *vmem(
                (FIELD, F32),
                (BASIS, BF16),
                (TRANSFER, BF16),
                (TURNED, BF16),
                (TURNED, BF16),
                (FIELD, BF16),
                ((8 * RANK, RANK), BF16),
                ((8 * RANK, RANK), BF16),
                ((8 * RANK, RANK), F32),
                ((8 * RANK, RANK), F32),
            ),
            *sems((6,)),
            pltpu.SemaphoreType.DMA,
        ],
        16,
    )(*in_hbm(leaf_live, right_hand, leaf_basis, leaf_transfer, up_turned, couple_turned))
    ra, rb, gathered = exchange(pa, pb, own, pair_up, out_path, 1)
    near, far = near_far(sb, pb, ra, rb)
    count = len(LEAF_BUFFERS)
    pa, pb, own, scal, sb, image = call(
        middle_kernel,
        [
            *PACKED,
            shape((RHS, 128), F32),
            pltpu.HBM(FIELD, BF16),
            pltpu.HBM(FIELD, F32),
        ],
        [VMEM] * 5 + [HBM] * (count + 1),
        [VMEM] * 4 + [HBM] * 2,
        [
            pltpu.SMEM((SLOTS,), jnp.int32),
            *vmem(*LEAF_BUFFERS, (FIELD, BF16), (FIELD, F32)),
            *sems((count + 1,), (1,), (4,)),
        ],
        16,
    )(
        ra, gathered, couple_zero, down_path, far,
        *in_hbm(leaf_live, leaf_transfer, leaf_basis, near, right_hand),
    )
    ra, rb, gathered = exchange(pa, pb, own, pair_up, out_path, 2)
    near, far = near_far(sb, pb, ra, rb)
    one, two, v, sent, scal = call(
        last_operator_kernel,
        [shape(FIELD, F32)] * 3 + [shape((DEVICES, 1, 128), F32), shape((RHS, 128), F32)],
        [VMEM] * 6 + [HBM] * (count + 2),
        [VMEM] * 5,
        [
            pltpu.SMEM((SLOTS,), jnp.int32),
            *vmem(*LEAF_BUFFERS, (FIELD, F32)),
            *sems((count + 2,)),
        ],
        16,
    )(
        ra, gathered, couple_zero, down_path, scal, far,
        *in_hbm(leaf_live, leaf_transfer, leaf_basis, near, right_hand, image),
    )
    gathered = lax.all_to_all(sent, "leaf", 0, 0)
    return call(
        final_kernel, [shape(FIELD, F32), shape((6, RHS), F32)], [VMEM] * 5, [VMEM] * 2, [], 8
    )(one, two, v, scal, gathered)


def solution(mesh):
    placed = (
        P("leaf", None, None),
        P("leaf"),
        P("leaf", None),
        P("leaf", None, None, None),
        P("leaf", None),
        P("leaf", None, None, None),
        P("leaf", None, None),
        P("leaf", None, None),
        P(),
        P(),
    )
    return jax.shard_map(
        on_device,
        mesh=mesh,
        in_specs=placed,
        out_specs=(P("leaf", None, None), P()),
        check_vma=False,
    )
```
